128 devices in a mesh: row: 8 (over y, core), col: 16 (over x, z).
Axes of the slice: x: 4, y: 4, z: 4, core: 2. Of those that a mesh axis runs over, the one named last changes fastest.
Arguments:
- tokens: bfloat16 [2048, 8192], P('col', 'row'), may hold values from -6 to 6
- gate_weight: bfloat16 [8192, 28672], P('row', 'col'), may hold values from -0.109375 to 0.109375
- up_weight: bfloat16 [8192, 28672], P('row', 'col'), may hold values from -0.109375 to 0.109375
- down_weight: bfloat16 [28672, 8192], P('col', 'row'), may hold values from -0.0546875 to 0.0546875
- gate_keep: int32 [224, 48], P('col'), may hold values from 0 to 63, as said below
- gate_count: int32 [224], P('col'), may hold values from 5 to 48, as said below
- up_keep: int32 [224, 48], P('col'), may hold values from 0 to 63, as said below
- up_count: int32 [224], P('col'), may hold values from 5 to 48, as said below
- down_keep: int32 [64, 176], P('row'), may hold values from 0 to 223, as said below
- down_count: int32 [64], P('row'), may hold values from 15 to 176, as said below
Outputs:
- output_rows: bfloat16 [2048, 8192], P('col', 'row')
The draws below stay inside these ranges and needn't reach their ends.
Inputs may be any that keep to these rules, and one draw needn't show every extreme that they name: `gate_keep`: each row holds distinct block indices of the model features. `gate_count`: some block column uses all 48 slots. `up_keep`: each row holds distinct block indices of the model features. `up_count`: some block column uses all 48 slots. `down_keep`: each row holds distinct block indices of the hidden units. `down_count`: some block column uses all 176 slots.
All inputs are finite; a program needn't handle non-finite values.
Results may differ from the reference program's by a relative error of at most 0.028.
Values may be sent and summed in bfloat16 or wider, within the bound.
A program may use at most 128 MiB of HBM per device.

```python
import jax
import jax.numpy as jnp
from jax import lax

D = 8192
FF = 28672
BLOCK = 128
KEEP_GU = 48
KEEP_DN = 176
TOKENS = 2048
N_ROW = 8
N_COL = 16


def keep_table(key, columns, blocks, most):
    keys = jax.random.split(key, columns)
    orders = jax.vmap(lambda sub_key: jax.random.permutation(sub_key, blocks))(keys)
    return orders[:, :most].astype(jnp.int32)


def keep_totals(key, columns, most):
    totals = jax.random.randint(key, (columns,), most // 12 + 1, most + 1)
    chosen = jax.random.randint(jax.random.fold_in(key, 7), (), 0, columns)
    return jnp.where(jnp.arange(columns) == chosen, most, totals).astype(jnp.int32)


def draw_gate_keep(key, part):
    return keep_table(jax.random.fold_in(key, 11), FF // BLOCK, D // BLOCK, KEEP_GU)


def draw_gate_count(key, part):
    return keep_totals(jax.random.fold_in(key, 12), FF // BLOCK, KEEP_GU)


def draw_up_keep(key, part):
    return keep_table(jax.random.fold_in(key, 21), FF // BLOCK, D // BLOCK, KEEP_GU)


def draw_up_count(key, part):
    return keep_totals(jax.random.fold_in(key, 22), FF // BLOCK, KEEP_GU)


def draw_down_keep(key, part):
    return keep_table(jax.random.fold_in(key, 31), D // BLOCK, FF // BLOCK, KEEP_DN)


def draw_down_count(key, part):
    return keep_totals(jax.random.fold_in(key, 32), D // BLOCK, KEEP_DN)


def block_scale(own_key, extent, cuts, low, largest):
    gain, own = 1.0, jax.random.fold_in(own_key, 6)
    for dim, shards_of in cuts:
        draws = jnp.exp(jax.random.uniform(jax.random.fold_in(own, dim), (shards_of,), jnp.float32, low / len(cuts), largest / len(cuts)))
        gain = gain * jnp.repeat(draws, extent[dim] // shards_of).reshape([-1 if axis == dim else 1 for axis in range(len(extent))])
    return gain


def noise(stream_key, dims, spread, reach, pieces=(), held_as=jnp.bfloat16):
    values = jax.random.normal(stream_key, dims, jnp.float32) * spread
    if len(pieces) > 0:
        values = block_scale(stream_key, dims, pieces, -0.22, 0.18) * values
    return jnp.clip(values, min=-reach, max=reach).astype(held_as)


def setup_inputs(seed: int = 0) -> dict:
    key_of = jax.random.split(jax.random.key(seed), 11)
    tokens = noise(key_of[0], (TOKENS, D), 1.0, 6.0, ((0, 16), (1, 8)))
    gate_weight = noise(key_of[1], (D, FF), (D * 2 // 5) ** -0.5, 0.109375, ((0, 8), (1, 16)))
    up_weight = noise(key_of[2], (D, FF), (D * 2 // 5) ** -0.5, 0.109375, ((0, 8), (1, 16)))
    down_weight = noise(key_of[3], (FF, D), (FF * 2 // 5) ** -0.5, 0.0546875, ((0, 16), (1, 8)))
    gate_keep = draw_gate_keep(jax.random.fold_in(key_of[10], 71), 0)
    gate_count = draw_gate_count(jax.random.fold_in(key_of[10], 71), 0)
    up_keep = draw_up_keep(jax.random.fold_in(key_of[10], 71), 0)
    up_count = draw_up_count(jax.random.fold_in(key_of[10], 71), 0)
    down_keep = draw_down_keep(jax.random.fold_in(key_of[10], 71), 0)
    down_count = draw_down_count(jax.random.fold_in(key_of[10], 71), 0)
    return dict(tokens=tokens, gate_weight=gate_weight, up_weight=up_weight, down_weight=down_weight, gate_keep=gate_keep, gate_count=gate_count, up_keep=up_keep, up_count=up_count, down_keep=down_keep, down_count=down_count)


def kept_blocks(keep_list, keep_count, blocks):
    position = jnp.arange(keep_list.shape[1], dtype=jnp.int32)
    active_slot = position[None, :] < keep_count[:, None]
    matches = (keep_list[:, :, None] == jnp.arange(blocks, dtype=jnp.int32)[None, None, :]) & active_slot[:, :, None]
    return jnp.any(matches, axis=1)


def expand_mask(block_mask, block_size):
    return jnp.repeat(jnp.repeat(block_mask, block_size, axis=0), block_size, axis=1)


def summed_ranges(left_matrix, right_matrix, ranges):
    range_width = left_matrix.shape[1] // ranges

    def add_range(running, piece_index):
        left_part = lax.dynamic_slice_in_dim(left_matrix, piece_index * range_width, range_width, 1)
        right_part = lax.dynamic_slice_in_dim(right_matrix, piece_index * range_width, range_width, 0)
        block_term = jnp.dot(left_part, right_part, preferred_element_type=jnp.float32)
        rounded = lax.optimization_barrier(block_term.astype(jnp.bfloat16))
        return running + rounded.astype(jnp.float32), None

    initial = jnp.zeros((left_matrix.shape[0], right_matrix.shape[1]), jnp.float32)
    return lax.scan(add_range, initial, jnp.arange(ranges, dtype=jnp.int32))[0]


def reference(tokens, gate_weight, up_weight, down_weight, gate_keep, gate_count, up_keep, up_count, down_keep, down_count):
    model_blocks = D // BLOCK
    hidden_blocks = FF // BLOCK
    zero_value = jnp.zeros((), jnp.bfloat16)
    gate_mask = expand_mask(kept_blocks(gate_keep, gate_count, model_blocks).T, BLOCK)
    up_mask = expand_mask(kept_blocks(up_keep, up_count, model_blocks).T, BLOCK)
    down_mask = expand_mask(kept_blocks(down_keep, down_count, hidden_blocks).T, BLOCK)
    gate_pruned = jnp.where(gate_mask, gate_weight, zero_value)
    up_pruned = jnp.where(up_mask, up_weight, zero_value)
    down_pruned = jnp.where(down_mask, down_weight, zero_value)
    gate_sums = summed_ranges(tokens, gate_pruned, N_ROW)
    up_sums = summed_ranges(tokens, up_pruned, N_ROW)
    hidden = (jax.nn.silu(gate_sums) * up_sums).astype(jnp.bfloat16)
    return summed_ranges(hidden, down_pruned, N_COL).astype(jnp.bfloat16)
```

```python
import jax
import jax.numpy as jnp
from jax import lax
from jax.sharding import PartitionSpec as P

BLOCK = 128
CHUNKS = 2
COL_A2A = True


def local_mask(keep_list, keep_count, offset, blocks):
    position = jnp.arange(keep_list.shape[1], dtype=jnp.int32)
    active_slot = position[None, :] < keep_count[:, None]
    local_index = keep_list - offset
    matches = (
        local_index[:, :, None] == jnp.arange(blocks, dtype=jnp.int32)[None, None, :]
    ) & active_slot[:, :, None]
    return jnp.any(matches, axis=1)


def apply_mask(weight, block_mask, block_size):
    block_rows, block_cols = block_mask.shape
    shaped = weight.reshape(block_rows, block_size, block_cols, block_size)
    masked = jnp.where(block_mask[:, None, :, None], shaped, jnp.zeros((), weight.dtype))
    return masked.reshape(weight.shape)


def on_device(
    tokens,
    gate_weight,
    up_weight,
    down_weight,
    gate_keep,
    gate_count,
    up_keep,
    up_count,
    down_keep,
    down_count,
):
    model_blocks = gate_weight.shape[0] // BLOCK
    hidden_blocks = gate_weight.shape[1] // BLOCK
    n_col = lax.axis_size("col")
    row_offset = lax.axis_index("row") * model_blocks
    col_offset = lax.axis_index("col") * hidden_blocks
    gate_pruned = apply_mask(
        gate_weight, local_mask(gate_keep, gate_count, row_offset, model_blocks).T, BLOCK
    )
    up_pruned = apply_mask(
        up_weight, local_mask(up_keep, up_count, row_offset, model_blocks).T, BLOCK
    )
    down_pruned = apply_mask(
        down_weight, local_mask(down_keep, down_count, col_offset, hidden_blocks).T, BLOCK
    )
    both_weights = jnp.concatenate([gate_pruned, up_pruned], axis=1)
    hidden_width = gate_weight.shape[1]
    rows = tokens.shape[0] // CHUNKS
    outs = []
    for k in range(CHUNKS):
        chunk = lax.all_gather(tokens[k * rows:(k + 1) * rows], "col", axis=0, tiled=True)
        partial_value = jnp.dot(chunk, both_weights, preferred_element_type=jnp.float32)
        summed = lax.psum_scatter(
            partial_value.astype(jnp.bfloat16), "row", scatter_dimension=0, tiled=True
        ).astype(jnp.float32)
        hidden = (
            jax.nn.silu(summed[:, :hidden_width]) * summed[:, hidden_width:]
        ).astype(jnp.bfloat16)
        hidden = lax.all_gather(hidden, "row", axis=0, tiled=True)
        terms = jnp.dot(hidden, down_pruned, preferred_element_type=jnp.float32).astype(
            jnp.bfloat16
        )
        if COL_A2A:
            terms = terms.reshape(n_col, rows, terms.shape[1])
            terms = lax.all_to_all(terms, "col", 0, 0, tiled=False)
            outs.append(jnp.sum(terms.astype(jnp.float32), axis=0).astype(jnp.bfloat16))
        else:
            outs.append(lax.psum_scatter(terms, "col", scatter_dimension=0, tiled=True))
    return jnp.concatenate(outs, axis=0)


def solution(mesh):
    return jax.shard_map(
        on_device,
        mesh=mesh,
        in_specs=(
            P("col", "row"),
            P("row", "col"),
            P("row", "col"),
            P("col", "row"),
            P("col", None),
            P("col"),
            P("col", None),
            P("col"),
            P("row", None),
            P("row"),
        ),
        out_specs=P("col", "row"),
        check_vma=False,
    )
```

```python
import jax
import jax.numpy as jnp
from jax import lax
from jax.sharding import PartitionSpec as P

BLOCK = 128
CHUNKS = 1
COL_A2A = True


def local_mask(keep_list, keep_count, offset, blocks):
    position = jnp.arange(keep_list.shape[1], dtype=jnp.int32)
    active_slot = position[None, :] < keep_count[:, None]
    local_index = keep_list - offset
    matches = (
        local_index[:, :, None] == jnp.arange(blocks, dtype=jnp.int32)[None, None, :]
    ) & active_slot[:, :, None]
    return jnp.any(matches, axis=1)


def apply_mask(weight, block_mask, block_size):
    block_rows, block_cols = block_mask.shape
    shaped = weight.reshape(block_rows, block_size, block_cols, block_size)
    masked = jnp.where(block_mask[:, None, :, None], shaped, jnp.zeros((), weight.dtype))
    return masked.reshape(weight.shape)


def row_perm(n_row, step):
    n_y = n_row // 2
    return [(y * 2 + c, ((y + step) % n_y) * 2 + c) for y in range(n_y) for c in range(2)]


def row_reduce_scatter(value, n_row):
    n_y = n_row // 2
    r = lax.axis_index("row")
    y = r // 2
    core = r % 2
    rows, width = value.shape
    halves = value.reshape(2, rows // 2, width)
    keep = lax.dynamic_index_in_dim(halves, core, 0, keepdims=False)
    send = lax.dynamic_index_in_dim(halves, 1 - core, 0, keepdims=False)
    swap = [(i, i ^ 1) for i in range(n_row)]
    pair = keep.astype(jnp.float32) + lax.ppermute(send, "row", swap).astype(jnp.float32)
    chunk = rows // 2 // n_y
    pair = pair.reshape(n_y, chunk, width)
    results = []
    for direction, cols in ((1, slice(0, width // 2)), (-1, slice(width // 2, width))):
        own = pair[:, :, cols]
        index = (y - direction) % n_y
        acc = lax.dynamic_index_in_dim(own, index, 0, keepdims=False)
        for step in range(n_y - 1):
            got = lax.ppermute(acc.astype(jnp.bfloat16), "row", row_perm(n_row, direction))
            index = (index - direction) % n_y
            acc = got.astype(jnp.float32) + lax.dynamic_index_in_dim(own, index, 0, keepdims=False)
        results.append(acc)
    return results


def row_all_gather(value, n_row):
    n_y = n_row // 2
    r = lax.axis_index("row")
    y = r // 2
    core = r % 2
    chunk, width = value.shape
    parts = []
    for direction, cols in ((1, slice(0, width // 2)), (-1, slice(width // 2, width))):
        held = value[:, cols]
        full = jnp.zeros((n_y, chunk, width // 2), value.dtype)
        full = lax.dynamic_update_index_in_dim(full, held, y, 0)
        for step in range(n_y - 1):
            held = lax.ppermute(held, "row", row_perm(n_row, direction))
            full = lax.dynamic_update_index_in_dim(full, held, (y - direction * (step + 1)) % n_y, 0)
        parts.append(full)
    half = jnp.concatenate(parts, axis=2).reshape(n_y * chunk, width)
    swap = [(i, i ^ 1) for i in range(n_row)]
    other = lax.ppermute(half, "row", swap)
    both = jnp.zeros((2, n_y * chunk, width), value.dtype)
    both = lax.dynamic_update_index_in_dim(both, half, core, 0)
    both = lax.dynamic_update_index_in_dim(both, other, 1 - core, 0)
    return both.reshape(2 * n_y * chunk, width)


def on_device(
    tokens,
    gate_weight,
    up_weight,
    down_weight,
    gate_keep,
    gate_count,
    up_keep,
    up_count,
    down_keep,
    down_count,
):
    model_blocks = gate_weight.shape[0] // BLOCK
    hidden_blocks = gate_weight.shape[1] // BLOCK
    n_col = lax.axis_size("col")
    n_row = lax.axis_size("row")
    row_offset = lax.axis_index("row") * model_blocks
    col_offset = lax.axis_index("col") * hidden_blocks
    gate_pruned = apply_mask(
        gate_weight, local_mask(gate_keep, gate_count, row_offset, model_blocks).T, BLOCK
    )
    up_pruned = apply_mask(
        up_weight, local_mask(up_keep, up_count, row_offset, model_blocks).T, BLOCK
    )
    down_pruned = apply_mask(
        down_weight, local_mask(down_keep, down_count, col_offset, hidden_blocks).T, BLOCK
    )
    both_weights = jnp.concatenate([gate_pruned, up_pruned], axis=1)
    rows = tokens.shape[0] // CHUNKS
    outs = []
    for k in range(CHUNKS):
        chunk = lax.all_gather(tokens[k * rows:(k + 1) * rows], "col", axis=0, tiled=True)
        partial_value = jnp.dot(chunk, both_weights, preferred_element_type=jnp.float32)
        gate_sums, up_sums = row_reduce_scatter(partial_value.astype(jnp.bfloat16), n_row)
        hidden = (jax.nn.silu(gate_sums) * up_sums).astype(jnp.bfloat16)
        hidden = row_all_gather(hidden, n_row)
        terms = jnp.dot(hidden, down_pruned, preferred_element_type=jnp.float32).astype(
            jnp.bfloat16
        )
        if COL_A2A:
            terms = terms.reshape(n_col, rows, terms.shape[1])
            terms = lax.all_to_all(terms, "col", 0, 0, tiled=False)
            outs.append(jnp.sum(terms.astype(jnp.float32), axis=0).astype(jnp.bfloat16))
        else:
            outs.append(lax.psum_scatter(terms, "col", scatter_dimension=0, tiled=True))
    return jnp.concatenate(outs, axis=0)


def solution(mesh):
    return jax.shard_map(
        on_device,
        mesh=mesh,
        in_specs=(
            P("col", "row"),
            P("row", "col"),
            P("row", "col"),
            P("col", "row"),
            P("col", None),
            P("col"),
            P("col", None),
            P("col"),
            P("row", None),
            P("row"),
        ),
        out_specs=P("col", "row"),
        check_vma=False,
    )
```

```python
import jax
import jax.numpy as jnp
from jax import lax
from jax.sharding import PartitionSpec as P

BLOCK = 128
CHUNKS = 2
COL_A2A = True


def local_mask(keep_list, keep_count, offset, blocks):
    position = jnp.arange(keep_list.shape[1], dtype=jnp.int32)
    active_slot = position[None, :] < keep_count[:, None]
    local_index = keep_list - offset
    matches = (
        local_index[:, :, None] == jnp.arange(blocks, dtype=jnp.int32)[None, None, :]
    ) & active_slot[:, :, None]
    return jnp.any(matches, axis=1)


def apply_mask(weight, block_mask, block_size):
    block_rows, block_cols = block_mask.shape
    shaped = weight.reshape(block_rows, block_size, block_cols, block_size)
    masked = jnp.where(block_mask[:, None, :, None], shaped, jnp.zeros((), weight.dtype))
    return masked.reshape(weight.shape)


def row_perm(n_row, step):
    n_y = n_row // 2
    return [(y * 2 + c, ((y + step) % n_y) * 2 + c) for y in range(n_y) for c in range(2)]


def row_reduce_scatter(tokens, weights, n_row):
    n_y = n_row // 2
    r = lax.axis_index("row")
    y = r // 2
    core = r % 2
    rows = tokens.shape[0]
    width = weights.shape[1]
    halves = tokens.reshape(2, rows // 2, tokens.shape[1])
    send = lax.dynamic_index_in_dim(halves, 1 - core, 0, keepdims=False)
    keep = lax.dynamic_index_in_dim(halves, core, 0, keepdims=False)
    send = jnp.dot(send, weights, preferred_element_type=jnp.float32).astype(jnp.bfloat16)
    swap = [(i, i ^ 1) for i in range(n_row)]
    got = lax.ppermute(send, "row", swap)
    keep = jnp.dot(keep, weights, preferred_element_type=jnp.float32).astype(jnp.bfloat16)
    pair = (keep.astype(jnp.float32) + got.astype(jnp.float32)).astype(jnp.bfloat16)
    chunk = rows // 2 // n_y
    pair = pair.reshape(n_y, chunk, width)
    results = []
    for direction, cols in ((1, slice(0, width // 2)), (-1, slice(width // 2, width))):
        own = pair[:, :, cols]
        index = (y - direction) % n_y
        acc = lax.dynamic_index_in_dim(own, index, 0, keepdims=False)
        for step in range(n_y - 1):
            got = lax.ppermute(acc.astype(jnp.bfloat16), "row", row_perm(n_row, direction))
            index = (index - direction) % n_y
            acc = got.astype(jnp.float32) + lax.dynamic_index_in_dim(own, index, 0, keepdims=False)
        results.append(acc)
    return results


def row_all_gather(value, n_row):
    n_y = n_row // 2
    r = lax.axis_index("row")
    y = r // 2
    core = r % 2
    chunk, width = value.shape
    parts = []
    for direction, cols in ((1, slice(0, width // 2)), (-1, slice(width // 2, width))):
        held = value[:, cols]
        full = jnp.zeros((n_y, chunk, width // 2), value.dtype)
        full = lax.dynamic_update_index_in_dim(full, held, y, 0)
        for step in range(n_y - 1):
            held = lax.ppermute(held, "row", row_perm(n_row, direction))
            full = lax.dynamic_update_index_in_dim(full, held, (y - direction * (step + 1)) % n_y, 0)
        parts.append(full)
    half = jnp.concatenate(parts, axis=2).reshape(n_y * chunk, width)
    swap = [(i, i ^ 1) for i in range(n_row)]
    other = lax.ppermute(half, "row", swap)
    both = jnp.zeros((2, n_y * chunk, width), value.dtype)
    both = lax.dynamic_update_index_in_dim(both, half, core, 0)
    both = lax.dynamic_update_index_in_dim(both, other, 1 - core, 0)
    return both.reshape(2 * n_y * chunk, width)


def on_device(
    tokens,
    gate_weight,
    up_weight,
    down_weight,
    gate_keep,
    gate_count,
    up_keep,
    up_count,
    down_keep,
    down_count,
):
    model_blocks = gate_weight.shape[0] // BLOCK
    hidden_blocks = gate_weight.shape[1] // BLOCK
    n_col = lax.axis_size("col")
    n_row = lax.axis_size("row")
    row_offset = lax.axis_index("row") * model_blocks
    col_offset = lax.axis_index("col") * hidden_blocks
    gate_pruned = apply_mask(
        gate_weight, local_mask(gate_keep, gate_count, row_offset, model_blocks).T, BLOCK
    )
    up_pruned = apply_mask(
        up_weight, local_mask(up_keep, up_count, row_offset, model_blocks).T, BLOCK
    )
    down_pruned = apply_mask(
        down_weight, local_mask(down_keep, down_count, col_offset, hidden_blocks).T, BLOCK
    )
    both_weights = jnp.concatenate([gate_pruned, up_pruned], axis=1)
    rows = tokens.shape[0] // CHUNKS
    outs = []
    for k in range(CHUNKS):
        chunk = lax.all_gather(tokens[k * rows:(k + 1) * rows], "col", axis=0, tiled=True)
        gate_sums, up_sums = row_reduce_scatter(chunk, both_weights, n_row)
        hidden = (jax.nn.silu(gate_sums) * up_sums).astype(jnp.bfloat16)
        hidden = row_all_gather(hidden, n_row)
        terms = jnp.dot(hidden, down_pruned, preferred_element_type=jnp.float32).astype(
            jnp.bfloat16
        )
        if COL_A2A:
            terms = terms.reshape(n_col, rows, terms.shape[1])
            terms = lax.all_to_all(terms, "col", 0, 0, tiled=False)
            outs.append(jnp.sum(terms.astype(jnp.float32), axis=0).astype(jnp.bfloat16))
        else:
            outs.append(lax.psum_scatter(terms, "col", scatter_dimension=0, tiled=True))
    return jnp.concatenate(outs, axis=0)


def solution(mesh):
    return jax.shard_map(
        on_device,
        mesh=mesh,
        in_specs=(
            P("col", "row"),
            P("row", "col"),
            P("row", "col"),
            P("col", "row"),
            P("col", None),
            P("col"),
            P("col", None),
            P("col"),
            P("row", None),
            P("row"),
        ),
        out_specs=P("col", "row"),
        check_vma=False,
    )
```

```python
import jax
import jax.numpy as jnp
from jax import lax
from jax.sharding import PartitionSpec as P

BLOCK = 128
CHUNKS = 2
COL_A2A = True
COL_RING = True


def local_mask(keep_list, keep_count, offset, blocks):
    position = jnp.arange(keep_list.shape[1], dtype=jnp.int32)
    active_slot = position[None, :] < keep_count[:, None]
    local_index = keep_list - offset
    matches = (
        local_index[:, :, None] == jnp.arange(blocks, dtype=jnp.int32)[None, None, :]
    ) & active_slot[:, :, None]
    return jnp.any(matches, axis=1)


def apply_mask(weight, block_mask, block_size):
    block_rows, block_cols = block_mask.shape
    shaped = weight.reshape(block_rows, block_size, block_cols, block_size)
    masked = jnp.where(block_mask[:, None, :, None], shaped, jnp.zeros((), weight.dtype))
    return masked.reshape(weight.shape)


def row_perm(n_row, step):
    n_y = n_row // 2
    return [(y * 2 + c, ((y + step) % n_y) * 2 + c) for y in range(n_y) for c in range(2)]


def row_reduce_scatter(tokens, weights, n_row, after):
    n_y = n_row // 2
    r = lax.axis_index("row")
    y = r // 2
    core = r % 2
    rows = tokens.shape[0]
    width = weights.shape[1]
    halves = tokens.reshape(2, rows // 2, tokens.shape[1])
    send = lax.dynamic_index_in_dim(halves, 1 - core, 0, keepdims=False)
    keep = lax.dynamic_index_in_dim(halves, core, 0, keepdims=False)
    send = jnp.dot(send, weights, preferred_element_type=jnp.float32).astype(jnp.bfloat16)
    swap = [(i, i ^ 1) for i in range(n_row)]
    got = lax.ppermute(send, "row", swap)
    keep = jnp.dot(keep, weights, preferred_element_type=jnp.float32).astype(jnp.bfloat16)
    pair = (keep.astype(jnp.float32) + got.astype(jnp.float32)).astype(jnp.bfloat16)
    if after is not None:
        pair, after = lax.optimization_barrier((pair, after))
    chunk = rows // 2 // n_y
    pair = pair.reshape(n_y, chunk, width)
    results = []
    for direction, cols in ((1, slice(0, width // 2)), (-1, slice(width // 2, width))):
        own = pair[:, :, cols]
        index = (y - direction) % n_y
        acc = lax.dynamic_index_in_dim(own, index, 0, keepdims=False)
        for step in range(n_y - 1):
            got = lax.ppermute(acc.astype(jnp.bfloat16), "row", row_perm(n_row, direction))
            index = (index - direction) % n_y
            acc = got.astype(jnp.float32) + lax.dynamic_index_in_dim(own, index, 0, keepdims=False)
        results.append(acc)
    return results


def row_all_gather(value, n_row):
    n_y = n_row // 2
    r = lax.axis_index("row")
    y = r // 2
    core = r % 2
    chunk, width = value.shape
    parts = []
    for direction, cols in ((1, slice(0, width // 2)), (-1, slice(width // 2, width))):
        held = value[:, cols]
        full = jnp.zeros((n_y, chunk, width // 2), value.dtype)
        full = lax.dynamic_update_index_in_dim(full, held, y, 0)
        for step in range(n_y - 1):
            held = lax.ppermute(held, "row", row_perm(n_row, direction))
            full = lax.dynamic_update_index_in_dim(full, held, (y - direction * (step + 1)) % n_y, 0)
        parts.append(full)
    half = jnp.concatenate(parts, axis=2).reshape(n_y * chunk, width)
    swap = [(i, i ^ 1) for i in range(n_row)]
    other = lax.ppermute(half, "row", swap)
    both = jnp.zeros((2, n_y * chunk, width), value.dtype)
    both = lax.dynamic_update_index_in_dim(both, half, core, 0)
    both = lax.dynamic_update_index_in_dim(both, other, 1 - core, 0)
    return both.reshape(2 * n_y * chunk, width)


def ring_reduce_scatter(own, pos, n, perm_of):
    width = own.shape[2]
    halves = []
    for direction, cols in ((1, slice(0, width // 2)), (-1, slice(width // 2, width))):
        part = own[:, :, cols]
        index = (pos - direction) % n
        acc = lax.dynamic_index_in_dim(part, index, 0, keepdims=False).astype(jnp.float32)
        for step in range(n - 1):
            got = lax.ppermute(acc.astype(jnp.bfloat16), "col", perm_of(direction))
            index = (index - direction) % n
            acc = got.astype(jnp.float32) + lax.dynamic_index_in_dim(part, index, 0, keepdims=False)
        halves.append(acc)
    return jnp.concatenate(halves, axis=1)


def col_reduce_scatter(terms, n_col):
    n_z = 4 if n_col % 4 == 0 else 1
    n_x = n_col // n_z
    c = lax.axis_index("col")
    x = c // n_z
    z = c % n_z
    rows, width = terms.shape

    def x_perm(d):
        return [(i * n_z + j, ((i + d) % n_x) * n_z + j) for i in range(n_x) for j in range(n_z)]

    def z_perm(d):
        return [(i * n_z + j, i * n_z + (j + d) % n_z) for i in range(n_x) for j in range(n_z)]

    part = ring_reduce_scatter(terms.reshape(n_x, rows // n_x, width), x, n_x, x_perm)
    part = part.astype(jnp.bfloat16).reshape(n_z, rows // n_x // n_z, width)
    return ring_reduce_scatter(part, z, n_z, z_perm).astype(jnp.bfloat16)


def on_device(
    tokens,
    gate_weight,
    up_weight,
    down_weight,
    gate_keep,
    gate_count,
    up_keep,
    up_count,
    down_keep,
    down_count,
):
    model_blocks = gate_weight.shape[0] // BLOCK
    hidden_blocks = gate_weight.shape[1] // BLOCK
    n_col = lax.axis_size("col")
    n_row = lax.axis_size("row")
    row_offset = lax.axis_index("row") * model_blocks
    col_offset = lax.axis_index("col") * hidden_blocks
    gate_pruned = apply_mask(
        gate_weight, local_mask(gate_keep, gate_count, row_offset, model_blocks).T, BLOCK
    )
    up_pruned = apply_mask(
        up_weight, local_mask(up_keep, up_count, row_offset, model_blocks).T, BLOCK
    )
    down_pruned = apply_mask(
        down_weight, local_mask(down_keep, down_count, col_offset, hidden_blocks).T, BLOCK
    )
    both_weights = jnp.concatenate([gate_pruned, up_pruned], axis=1)
    rows = tokens.shape[0] // CHUNKS
    gathered = lax.all_gather(tokens, "col", axis=0, tiled=True)
    gathered = gathered.reshape(n_col, CHUNKS, rows, gathered.shape[1])
    outs = []
    previous = None
    for k in range(CHUNKS):
        chunk = gathered[:, k].reshape(n_col * rows, gathered.shape[3])
        gate_sums, up_sums = row_reduce_scatter(chunk, both_weights, n_row, previous)
        hidden = (jax.nn.silu(gate_sums) * up_sums).astype(jnp.bfloat16)
        hidden = row_all_gather(hidden, n_row)
        terms = jnp.dot(hidden, down_pruned, preferred_element_type=jnp.float32).astype(
            jnp.bfloat16
        )
        previous = terms
        if COL_RING:
            outs.append(col_reduce_scatter(terms, n_col))
        elif COL_A2A:
            terms = terms.reshape(n_col, rows, terms.shape[1])
            terms = lax.all_to_all(terms, "col", 0, 0, tiled=False)
            outs.append(jnp.sum(terms.astype(jnp.float32), axis=0).astype(jnp.bfloat16))
        else:
            outs.append(lax.psum_scatter(terms, "col", scatter_dimension=0, tiled=True))
    return jnp.concatenate(outs, axis=0)


def solution(mesh):
    return jax.shard_map(
        on_device,
        mesh=mesh,
        in_specs=(
            P("col", "row"),
            P("row", "col"),
            P("row", "col"),
            P("col", "row"),
            P("col", None),
            P("col"),
            P("col", None),
            P("col"),
            P("row", None),
            P("row"),
        ),
        out_specs=P("col", "row"),
        check_vma=False,
    )
```

```python
import jax
import jax.numpy as jnp
from jax import lax
from jax.sharding import PartitionSpec as P

BLOCK = 128
CHUNKS = 2
COL_A2A = True
COL_RING = True


def local_mask(keep_list, keep_count, offset, blocks):
    position = jnp.arange(keep_list.shape[1], dtype=jnp.int32)
    active_slot = position[None, :] < keep_count[:, None]
    local_index = keep_list - offset
    matches = (
        local_index[:, :, None] == jnp.arange(blocks, dtype=jnp.int32)[None, None, :]
    ) & active_slot[:, :, None]
    return jnp.any(matches, axis=1)


def apply_mask(weight, block_mask, block_size):
    block_rows, block_cols = block_mask.shape
    shaped = weight.reshape(block_rows, block_size, block_cols, block_size)
    masked = jnp.where(block_mask[:, None, :, None], shaped, jnp.zeros((), weight.dtype))
    return masked.reshape(weight.shape)


def row_perm(n_row, step):
    n_y = n_row // 2
    return [(y * 2 + c, ((y + step) % n_y) * 2 + c) for y in range(n_y) for c in range(2)]


def row_reduce_scatter(tokens, weights, n_row, after):
    n_y = n_row // 2
    r = lax.axis_index("row")
    y = r // 2
    core = r % 2
    rows = tokens.shape[0]
    width = weights.shape[1]
    halves = tokens.reshape(2, rows // 2, tokens.shape[1])
    send = lax.dynamic_index_in_dim(halves, 1 - core, 0, keepdims=False)
    keep = lax.dynamic_index_in_dim(halves, core, 0, keepdims=False)
    send = jnp.dot(send, weights, preferred_element_type=jnp.float32).astype(jnp.bfloat16)
    swap = [(i, i ^ 1) for i in range(n_row)]
    got = lax.ppermute(send, "row", swap)
    keep = jnp.dot(keep, weights, preferred_element_type=jnp.float32).astype(jnp.bfloat16)
    pair = (keep.astype(jnp.float32) + got.astype(jnp.float32)).astype(jnp.bfloat16)
    if after is not None:
        pair, after = lax.optimization_barrier((pair, after))
    chunk = rows // 2 // n_y
    pair = pair.reshape(n_y, chunk, width)
    results = []
    for direction, cols in ((1, slice(0, width // 2)), (-1, slice(width // 2, width))):
        own = pair[:, :, cols]
        index = (y - direction) % n_y
        acc = lax.dynamic_index_in_dim(own, index, 0, keepdims=False)
        for step in range(n_y - 1):
            got = lax.ppermute(acc.astype(jnp.bfloat16), "row", row_perm(n_row, direction))
            index = (index - direction) % n_y
            acc = got.astype(jnp.float32) + lax.dynamic_index_in_dim(own, index, 0, keepdims=False)
        results.append(acc)
    return results


def row_all_gather(value, n_row):
    n_y = n_row // 2
    r = lax.axis_index("row")
    y = r // 2
    core = r % 2
    chunk, width = value.shape
    parts = []
    for direction, cols in ((1, slice(0, width // 2)), (-1, slice(width // 2, width))):
        held = value[:, cols]
        full = jnp.zeros((n_y, chunk, width // 2), value.dtype)
        full = lax.dynamic_update_index_in_dim(full, held, y, 0)
        for step in range(n_y - 1):
            held = lax.ppermute(held, "row", row_perm(n_row, direction))
            full = lax.dynamic_update_index_in_dim(full, held, (y - direction * (step + 1)) % n_y, 0)
        parts.append(full)
    half = jnp.concatenate(parts, axis=2).reshape(n_y * chunk, width)
    swap = [(i, i ^ 1) for i in range(n_row)]
    other = lax.ppermute(half, "row", swap)
    both = jnp.zeros((2, n_y * chunk, width), value.dtype)
    both = lax.dynamic_update_index_in_dim(both, half, core, 0)
    both = lax.dynamic_update_index_in_dim(both, other, 1 - core, 0)
    return both.reshape(2 * n_y * chunk, width)


def ring_reduce_scatter(own, pos, n, perm_of):
    width = own.shape[2]
    halves = []
    for direction, cols in ((1, slice(0, width // 2)), (-1, slice(width // 2, width))):
        part = own[:, :, cols]
        index = (pos - direction) % n
        acc = lax.dynamic_index_in_dim(part, index, 0, keepdims=False).astype(jnp.float32)
        for step in range(n - 1):
            got = lax.ppermute(acc.astype(jnp.bfloat16), "col", perm_of(direction))
            index = (index - direction) % n
            acc = got.astype(jnp.float32) + lax.dynamic_index_in_dim(part, index, 0, keepdims=False)
        halves.append(acc)
    return jnp.concatenate(halves, axis=1)


def ring_all_gather(value, pos, n, perm_of):
    chunk, width = value.shape
    parts = []
    for direction, cols in ((1, slice(0, width // 2)), (-1, slice(width // 2, width))):
        held = value[:, cols]
        full = jnp.zeros((n, chunk, width // 2), value.dtype)
        full = lax.dynamic_update_index_in_dim(full, held, pos, 0)
        for step in range(n - 1):
            held = lax.ppermute(held, "col", perm_of(direction))
            full = lax.dynamic_update_index_in_dim(full, held, (pos - direction * (step + 1)) % n, 0)
        parts.append(full)
    return jnp.concatenate(parts, axis=2)


def col_axes(n_col):
    n_z = 4 if n_col % 4 == 0 else 1
    n_x = n_col // n_z
    c = lax.axis_index("col")

    def x_perm(d):
        return [(i * n_z + j, ((i + d) % n_x) * n_z + j) for i in range(n_x) for j in range(n_z)]

    def z_perm(d):
        return [(i * n_z + j, i * n_z + (j + d) % n_z) for i in range(n_x) for j in range(n_z)]

    return n_x, n_z, c // n_z, c % n_z, x_perm, z_perm


def col_all_gather(value, n_col):
    n_x, n_z, x, z, x_perm, z_perm = col_axes(n_col)
    rows, width = value.shape
    part = ring_all_gather(value, z, n_z, z_perm).reshape(n_z * rows, width)
    return ring_all_gather(part, x, n_x, x_perm).reshape(n_x * n_z * rows, width)


def col_reduce_scatter(terms, n_col):
    n_z = 4 if n_col % 4 == 0 else 1
    n_x = n_col // n_z
    c = lax.axis_index("col")
    x = c // n_z
    z = c % n_z
    rows, width = terms.shape

    def x_perm(d):
        return [(i * n_z + j, ((i + d) % n_x) * n_z + j) for i in range(n_x) for j in range(n_z)]

    def z_perm(d):
        return [(i * n_z + j, i * n_z + (j + d) % n_z) for i in range(n_x) for j in range(n_z)]

    part = ring_reduce_scatter(terms.reshape(n_x, rows // n_x, width), x, n_x, x_perm)
    part = part.astype(jnp.bfloat16).reshape(n_z, rows // n_x // n_z, width)
    return ring_reduce_scatter(part, z, n_z, z_perm).astype(jnp.bfloat16)


def on_device(
    tokens,
    gate_weight,
    up_weight,
    down_weight,
    gate_keep,
    gate_count,
    up_keep,
    up_count,
    down_keep,
    down_count,
):
    model_blocks = gate_weight.shape[0] // BLOCK
    hidden_blocks = gate_weight.shape[1] // BLOCK
    n_col = lax.axis_size("col")
    n_row = lax.axis_size("row")
    row_offset = lax.axis_index("row") * model_blocks
    col_offset = lax.axis_index("col") * hidden_blocks
    gate_pruned = apply_mask(
        gate_weight, local_mask(gate_keep, gate_count, row_offset, model_blocks).T, BLOCK
    )
    up_pruned = apply_mask(
        up_weight, local_mask(up_keep, up_count, row_offset, model_blocks).T, BLOCK
    )
    down_pruned = apply_mask(
        down_weight, local_mask(down_keep, down_count, col_offset, hidden_blocks).T, BLOCK
    )
    both_weights = jnp.concatenate([gate_pruned, up_pruned], axis=1)
    rows = tokens.shape[0] // CHUNKS
    gathered = col_all_gather(tokens, n_col)
    gathered = gathered.reshape(n_col, CHUNKS, rows, gathered.shape[1])
    outs = []
    previous = None
    for k in range(CHUNKS):
        chunk = gathered[:, k].reshape(n_col * rows, gathered.shape[3])
        gate_sums, up_sums = row_reduce_scatter(chunk, both_weights, n_row, previous)
        hidden = (jax.nn.silu(gate_sums) * up_sums).astype(jnp.bfloat16)
        hidden = row_all_gather(hidden, n_row)
        terms = jnp.dot(hidden, down_pruned, preferred_element_type=jnp.float32).astype(
            jnp.bfloat16
        )
        previous = terms
        if COL_RING:
            outs.append(col_reduce_scatter(terms, n_col))
        elif COL_A2A:
            terms = terms.reshape(n_col, rows, terms.shape[1])
            terms = lax.all_to_all(terms, "col", 0, 0, tiled=False)
            outs.append(jnp.sum(terms.astype(jnp.float32), axis=0).astype(jnp.bfloat16))
        else:
            outs.append(lax.psum_scatter(terms, "col", scatter_dimension=0, tiled=True))
    return jnp.concatenate(outs, axis=0)


def solution(mesh):
    return jax.shard_map(
        on_device,
        mesh=mesh,
        in_specs=(
            P("col", "row"),
            P("row", "col"),
            P("row", "col"),
            P("col", "row"),
            P("col", None),
            P("col"),
            P("col", None),
            P("col"),
            P("row", None),
            P("row"),
        ),
        out_specs=P("col", "row"),
        check_vma=False,
    )
```

```python
import jax
import jax.numpy as jnp
from jax import lax
from jax.sharding import PartitionSpec as P

BLOCK = 128
CHUNKS = 1
COL_A2A = True
COL_RING = True


def local_mask(keep_list, keep_count, offset, blocks):
    position = jnp.arange(keep_list.shape[1], dtype=jnp.int32)
    active_slot = position[None, :] < keep_count[:, None]
    local_index = keep_list - offset
    matches = (
        local_index[:, :, None] == jnp.arange(blocks, dtype=jnp.int32)[None, None, :]
    ) & active_slot[:, :, None]
    return jnp.any(matches, axis=1)


def apply_mask(weight, block_mask, block_size):
    block_rows, block_cols = block_mask.shape
    shaped = weight.reshape(block_rows, block_size, block_cols, block_size)
    masked = jnp.where(block_mask[:, None, :, None], shaped, jnp.zeros((), weight.dtype))
    return masked.reshape(weight.shape)


def row_perm(n_row, step):
    n_y = n_row // 2
    return [(y * 2 + c, ((y + step) % n_y) * 2 + c) for y in range(n_y) for c in range(2)]


def row_reduce_scatter(tokens, weights, n_row, after):
    n_y = n_row // 2
    r = lax.axis_index("row")
    y = r // 2
    core = r % 2
    rows = tokens.shape[0]
    width = weights.shape[1]
    halves = tokens.reshape(2, rows // 2, tokens.shape[1])
    send = lax.dynamic_index_in_dim(halves, 1 - core, 0, keepdims=False)
    keep = lax.dynamic_index_in_dim(halves, core, 0, keepdims=False)
    send = jnp.dot(send, weights, preferred_element_type=jnp.float32).astype(jnp.bfloat16)
    swap = [(i, i ^ 1) for i in range(n_row)]
    got = lax.ppermute(send, "row", swap)
    keep = jnp.dot(keep, weights, preferred_element_type=jnp.float32).astype(jnp.bfloat16)
    pair = (keep.astype(jnp.float32) + got.astype(jnp.float32)).astype(jnp.bfloat16)
    if after is not None:
        pair, after = lax.optimization_barrier((pair, after))
    chunk = rows // 2 // n_y
    pair = pair.reshape(n_y, chunk, width)
    results = []
    for direction, cols in ((1, slice(0, width // 2)), (-1, slice(width // 2, width))):
        own = pair[:, :, cols]
        index = (y - direction) % n_y
        acc = lax.dynamic_index_in_dim(own, index, 0, keepdims=False)
        for step in range(n_y - 1):
            got = lax.ppermute(acc.astype(jnp.bfloat16), "row", row_perm(n_row, direction))
            index = (index - direction) % n_y
            acc = got.astype(jnp.float32) + lax.dynamic_index_in_dim(own, index, 0, keepdims=False)
        results.append(acc)
    return results


def row_all_gather(value, n_row):
    n_y = n_row // 2
    r = lax.axis_index("row")
    y = r // 2
    core = r % 2
    chunk, width = value.shape
    parts = []
    for direction, cols in ((1, slice(0, width // 2)), (-1, slice(width // 2, width))):
        held = value[:, cols]
        full = jnp.zeros((n_y, chunk, width // 2), value.dtype)
        full = lax.dynamic_update_index_in_dim(full, held, y, 0)
        for step in range(n_y - 1):
            held = lax.ppermute(held, "row", row_perm(n_row, direction))
            full = lax.dynamic_update_index_in_dim(full, held, (y - direction * (step + 1)) % n_y, 0)
        parts.append(full)
    half = jnp.concatenate(parts, axis=2).reshape(n_y * chunk, width)
    swap = [(i, i ^ 1) for i in range(n_row)]
    other = lax.ppermute(half, "row", swap)
    both = jnp.zeros((2, n_y * chunk, width), value.dtype)
    both = lax.dynamic_update_index_in_dim(both, half, core, 0)
    both = lax.dynamic_update_index_in_dim(both, other, 1 - core, 0)
    return both.reshape(2 * n_y * chunk, width)


def ring_reduce_scatter(own, pos, n, perm_of):
    width = own.shape[2]
    halves = []
    for direction, cols in ((1, slice(0, width // 2)), (-1, slice(width // 2, width))):
        part = own[:, :, cols]
        index = (pos - direction) % n
        acc = lax.dynamic_index_in_dim(part, index, 0, keepdims=False).astype(jnp.float32)
        for step in range(n - 1):
            got = lax.ppermute(acc.astype(jnp.bfloat16), "col", perm_of(direction))
            index = (index - direction) % n
            acc = got.astype(jnp.float32) + lax.dynamic_index_in_dim(part, index, 0, keepdims=False)
        halves.append(acc)
    return jnp.concatenate(halves, axis=1)


def ring_all_gather(value, pos, n, perm_of):
    chunk, width = value.shape
    parts = []
    for direction, cols in ((1, slice(0, width // 2)), (-1, slice(width // 2, width))):
        held = value[:, cols]
        full = jnp.zeros((n, chunk, width // 2), value.dtype)
        full = lax.dynamic_update_index_in_dim(full, held, pos, 0)
        for step in range(n - 1):
            held = lax.ppermute(held, "col", perm_of(direction))
            full = lax.dynamic_update_index_in_dim(full, held, (pos - direction * (step + 1)) % n, 0)
        parts.append(full)
    return jnp.concatenate(parts, axis=2)


def col_axes(n_col):
    n_z = 4 if n_col % 4 == 0 else 1
    n_x = n_col // n_z
    c = lax.axis_index("col")

    def x_perm(d):
        return [(i * n_z + j, ((i + d) % n_x) * n_z + j) for i in range(n_x) for j in range(n_z)]

    def z_perm(d):
        return [(i * n_z + j, i * n_z + (j + d) % n_z) for i in range(n_x) for j in range(n_z)]

    return n_x, n_z, c // n_z, c % n_z, x_perm, z_perm


def col_all_gather(value, n_col):
    n_x, n_z, x, z, x_perm, z_perm = col_axes(n_col)
    rows, width = value.shape
    part = ring_all_gather(value, z, n_z, z_perm).reshape(n_z * rows, width)
    return ring_all_gather(part, x, n_x, x_perm).reshape(n_x * n_z * rows, width)


def col_reduce_scatter(terms, n_col):
    n_z = 4 if n_col % 4 == 0 else 1
    n_x = n_col // n_z
    c = lax.axis_index("col")
    x = c // n_z
    z = c % n_z
    rows, width = terms.shape

    def x_perm(d):
        return [(i * n_z + j, ((i + d) % n_x) * n_z + j) for i in range(n_x) for j in range(n_z)]

    def z_perm(d):
        return [(i * n_z + j, i * n_z + (j + d) % n_z) for i in range(n_x) for j in range(n_z)]

    part = ring_reduce_scatter(terms.reshape(n_x, rows // n_x, width), x, n_x, x_perm)
    part = part.astype(jnp.bfloat16).reshape(n_z, rows // n_x // n_z, width)
    return ring_reduce_scatter(part, z, n_z, z_perm).astype(jnp.bfloat16)


def on_device(
    tokens,
    gate_weight,
    up_weight,
    down_weight,
    gate_keep,
    gate_count,
    up_keep,
    up_count,
    down_keep,
    down_count,
):
    model_blocks = gate_weight.shape[0] // BLOCK
    hidden_blocks = gate_weight.shape[1] // BLOCK
    n_col = lax.axis_size("col")
    n_row = lax.axis_size("row")
    row_offset = lax.axis_index("row") * model_blocks
    col_offset = lax.axis_index("col") * hidden_blocks
    gate_pruned = apply_mask(
        gate_weight, local_mask(gate_keep, gate_count, row_offset, model_blocks).T, BLOCK
    )
    up_pruned = apply_mask(
        up_weight, local_mask(up_keep, up_count, row_offset, model_blocks).T, BLOCK
    )
    down_pruned = apply_mask(
        down_weight, local_mask(down_keep, down_count, col_offset, hidden_blocks).T, BLOCK
    )
    both_weights = jnp.concatenate([gate_pruned, up_pruned], axis=1)
    rows = tokens.shape[0] // CHUNKS
    gathered = col_all_gather(tokens, n_col)
    gathered = gathered.reshape(n_col, CHUNKS, rows, gathered.shape[1])
    outs = []
    previous = None
    for k in range(CHUNKS):
        chunk = gathered[:, k].reshape(n_col * rows, gathered.shape[3])
        gate_sums, up_sums = row_reduce_scatter(chunk, both_weights, n_row, previous)
        hidden = (jax.nn.silu(gate_sums) * up_sums).astype(jnp.bfloat16)
        hidden = row_all_gather(hidden, n_row)
        terms = jnp.dot(hidden, down_pruned, preferred_element_type=jnp.float32).astype(
            jnp.bfloat16
        )
        previous = terms
        if COL_RING:
            outs.append(col_reduce_scatter(terms, n_col))
        elif COL_A2A:
            terms = terms.reshape(n_col, rows, terms.shape[1])
            terms = lax.all_to_all(terms, "col", 0, 0, tiled=False)
            outs.append(jnp.sum(terms.astype(jnp.float32), axis=0).astype(jnp.bfloat16))
        else:
            outs.append(lax.psum_scatter(terms, "col", scatter_dimension=0, tiled=True))
    return jnp.concatenate(outs, axis=0)


def solution(mesh):
    return jax.shard_map(
        on_device,
        mesh=mesh,
        in_specs=(
            P("col", "row"),
            P("row", "col"),
            P("row", "col"),
            P("col", "row"),
            P("col", None),
            P("col"),
            P("col", None),
            P("col"),
            P("row", None),
            P("row"),
        ),
        out_specs=P("col", "row"),
        check_vma=False,
    )
```

```python
import jax
import jax.numpy as jnp
from jax import lax
from jax.sharding import PartitionSpec as P

BLOCK = 128
CHUNKS = 1
COL_A2A = True
COL_RING = False


def local_mask(keep_list, keep_count, offset, blocks):
    position = jnp.arange(keep_list.shape[1], dtype=jnp.int32)
    active_slot = position[None, :] < keep_count[:, None]
    local_index = keep_list - offset
    matches = (
        local_index[:, :, None] == jnp.arange(blocks, dtype=jnp.int32)[None, None, :]
    ) & active_slot[:, :, None]
    return jnp.any(matches, axis=1)


def apply_mask(weight, block_mask, block_size):
    block_rows, block_cols = block_mask.shape
    shaped = weight.reshape(block_rows, block_size, block_cols, block_size)
    masked = jnp.where(block_mask[:, None, :, None], shaped, jnp.zeros((), weight.dtype))
    return masked.reshape(weight.shape)


def row_perm(n_row, step):
    n_y = n_row // 2
    return [(y * 2 + c, ((y + step) % n_y) * 2 + c) for y in range(n_y) for c in range(2)]


def row_reduce_scatter(tokens, weights, n_row, after):
    n_y = n_row // 2
    r = lax.axis_index("row")
    y = r // 2
    core = r % 2
    rows = tokens.shape[0]
    width = weights.shape[1]
    halves = tokens.reshape(2, rows // 2, tokens.shape[1])
    send = lax.dynamic_index_in_dim(halves, 1 - core, 0, keepdims=False)
    keep = lax.dynamic_index_in_dim(halves, core, 0, keepdims=False)
    send = jnp.dot(send, weights, preferred_element_type=jnp.float32).astype(jnp.bfloat16)
    swap = [(i, i ^ 1) for i in range(n_row)]
    got = lax.ppermute(send, "row", swap)
    keep = jnp.dot(keep, weights, preferred_element_type=jnp.float32).astype(jnp.bfloat16)
    pair = (keep.astype(jnp.float32) + got.astype(jnp.float32)).astype(jnp.bfloat16)
    if after is not None:
        pair, after = lax.optimization_barrier((pair, after))
    chunk = rows // 2 // n_y
    pair = pair.reshape(n_y, chunk, width)
    results = []
    for direction, cols in ((1, slice(0, width // 2)), (-1, slice(width // 2, width))):
        own = pair[:, :, cols]
        index = (y - direction) % n_y
        acc = lax.dynamic_index_in_dim(own, index, 0, keepdims=False)
        for step in range(n_y - 1):
            got = lax.ppermute(acc.astype(jnp.bfloat16), "row", row_perm(n_row, direction))
            index = (index - direction) % n_y
            acc = got.astype(jnp.float32) + lax.dynamic_index_in_dim(own, index, 0, keepdims=False)
        results.append(acc)
    return results


def row_all_gather(value, n_row):
    n_y = n_row // 2
    r = lax.axis_index("row")
    y = r // 2
    core = r % 2
    chunk, width = value.shape
    parts = []
    for direction, cols in ((1, slice(0, width // 2)), (-1, slice(width // 2, width))):
        held = value[:, cols]
        full = jnp.zeros((n_y, chunk, width // 2), value.dtype)
        full = lax.dynamic_update_index_in_dim(full, held, y, 0)
        for step in range(n_y - 1):
            held = lax.ppermute(held, "row", row_perm(n_row, direction))
            full = lax.dynamic_update_index_in_dim(full, held, (y - direction * (step + 1)) % n_y, 0)
        parts.append(full)
    half = jnp.concatenate(parts, axis=2).reshape(n_y * chunk, width)
    swap = [(i, i ^ 1) for i in range(n_row)]
    other = lax.ppermute(half, "row", swap)
    both = jnp.zeros((2, n_y * chunk, width), value.dtype)
    both = lax.dynamic_update_index_in_dim(both, half, core, 0)
    both = lax.dynamic_update_index_in_dim(both, other, 1 - core, 0)
    return both.reshape(2 * n_y * chunk, width)


def ring_reduce_scatter(own, pos, n, perm_of):
    width = own.shape[2]
    halves = []
    for direction, cols in ((1, slice(0, width // 2)), (-1, slice(width // 2, width))):
        part = own[:, :, cols]
        index = (pos - direction) % n
        acc = lax.dynamic_index_in_dim(part, index, 0, keepdims=False).astype(jnp.float32)
        for step in range(n - 1):
            got = lax.ppermute(acc.astype(jnp.bfloat16), "col", perm_of(direction))
            index = (index - direction) % n
            acc = got.astype(jnp.float32) + lax.dynamic_index_in_dim(part, index, 0, keepdims=False)
        halves.append(acc)
    return jnp.concatenate(halves, axis=1)


def ring_all_gather(value, pos, n, perm_of):
    chunk, width = value.shape
    parts = []
    for direction, cols in ((1, slice(0, width // 2)), (-1, slice(width // 2, width))):
        held = value[:, cols]
        full = jnp.zeros((n, chunk, width // 2), value.dtype)
        full = lax.dynamic_update_index_in_dim(full, held, pos, 0)
        for step in range(n - 1):
            held = lax.ppermute(held, "col", perm_of(direction))
            full = lax.dynamic_update_index_in_dim(full, held, (pos - direction * (step + 1)) % n, 0)
        parts.append(full)
    return jnp.concatenate(parts, axis=2)


def col_axes(n_col):
    n_z = 4 if n_col % 4 == 0 else 1
    n_x = n_col // n_z
    c = lax.axis_index("col")

    def x_perm(d):
        return [(i * n_z + j, ((i + d) % n_x) * n_z + j) for i in range(n_x) for j in range(n_z)]

    def z_perm(d):
        return [(i * n_z + j, i * n_z + (j + d) % n_z) for i in range(n_x) for j in range(n_z)]

    return n_x, n_z, c // n_z, c % n_z, x_perm, z_perm


def col_all_gather(value, n_col):
    n_x, n_z, x, z, x_perm, z_perm = col_axes(n_col)
    rows, width = value.shape
    part = ring_all_gather(value, z, n_z, z_perm).reshape(n_z * rows, width)
    return ring_all_gather(part, x, n_x, x_perm).reshape(n_x * n_z * rows, width)


def col_reduce_scatter(terms, n_col):
    n_z = 4 if n_col % 4 == 0 else 1
    n_x = n_col // n_z
    c = lax.axis_index("col")
    x = c // n_z
    z = c % n_z
    rows, width = terms.shape

    def x_perm(d):
        return [(i * n_z + j, ((i + d) % n_x) * n_z + j) for i in range(n_x) for j in range(n_z)]

    def z_perm(d):
        return [(i * n_z + j, i * n_z + (j + d) % n_z) for i in range(n_x) for j in range(n_z)]

    part = ring_reduce_scatter(terms.reshape(n_x, rows // n_x, width), x, n_x, x_perm)
    part = part.astype(jnp.bfloat16).reshape(n_z, rows // n_x // n_z, width)
    return ring_reduce_scatter(part, z, n_z, z_perm).astype(jnp.bfloat16)


def on_device(
    tokens,
    gate_weight,
    up_weight,
    down_weight,
    gate_keep,
    gate_count,
    up_keep,
    up_count,
    down_keep,
    down_count,
):
    model_blocks = gate_weight.shape[0] // BLOCK
    hidden_blocks = gate_weight.shape[1] // BLOCK
    n_col = lax.axis_size("col")
    n_row = lax.axis_size("row")
    row_offset = lax.axis_index("row") * model_blocks
    col_offset = lax.axis_index("col") * hidden_blocks
    gate_pruned = apply_mask(
        gate_weight, local_mask(gate_keep, gate_count, row_offset, model_blocks).T, BLOCK
    )
    up_pruned = apply_mask(
        up_weight, local_mask(up_keep, up_count, row_offset, model_blocks).T, BLOCK
    )
    down_pruned = apply_mask(
        down_weight, local_mask(down_keep, down_count, col_offset, hidden_blocks).T, BLOCK
    )
    both_weights = jnp.concatenate([gate_pruned, up_pruned], axis=1)
    rows = tokens.shape[0] // CHUNKS
    gathered = lax.all_gather(tokens, "col", axis=0, tiled=True)
    gathered = gathered.reshape(n_col, CHUNKS, rows, gathered.shape[1])
    outs = []
    previous = None
    for k in range(CHUNKS):
        chunk = gathered[:, k].reshape(n_col * rows, gathered.shape[3])
        gate_sums, up_sums = row_reduce_scatter(chunk, both_weights, n_row, previous)
        hidden = (jax.nn.silu(gate_sums) * up_sums).astype(jnp.bfloat16)
        hidden = row_all_gather(hidden, n_row)
        terms = jnp.dot(hidden, down_pruned, preferred_element_type=jnp.float32).astype(
            jnp.bfloat16
        )
        previous = terms
        if COL_RING:
            outs.append(col_reduce_scatter(terms, n_col))
        elif COL_A2A and k == CHUNKS - 1:
            terms = terms.reshape(n_col, rows, terms.shape[1])
            terms = lax.all_to_all(terms, "col", 0, 0, tiled=False)
            outs.append(jnp.sum(terms.astype(jnp.float32), axis=0).astype(jnp.bfloat16))
        else:
            outs.append(lax.psum_scatter(terms, "col", scatter_dimension=0, tiled=True))
    return jnp.concatenate(outs, axis=0)


def solution(mesh):
    return jax.shard_map(
        on_device,
        mesh=mesh,
        in_specs=(
            P("col", "row"),
            P("row", "col"),
            P("row", "col"),
            P("col", "row"),
            P("col", None),
            P("col"),
            P("col", None),
            P("col"),
            P("row", None),
            P("row"),
        ),
        out_specs=P("col", "row"),
        check_vma=False,
    )
```

```python
import jax
import jax.numpy as jnp
from jax import lax
from jax.sharding import PartitionSpec as P

BLOCK = 128
CHUNKS = 1
COL_A2A = True
COL_RING = False


def local_mask(keep_list, keep_count, offset, blocks):
    position = jnp.arange(keep_list.shape[1], dtype=jnp.int32)
    active_slot = position[None, :] < keep_count[:, None]
    local_index = keep_list - offset
    matches = (
        local_index[:, :, None] == jnp.arange(blocks, dtype=jnp.int32)[None, None, :]
    ) & active_slot[:, :, None]
    return jnp.any(matches, axis=1)


def apply_mask(weight, block_mask, block_size):
    block_rows, block_cols = block_mask.shape
    shaped = weight.reshape(block_rows, block_size, block_cols, block_size)
    masked = jnp.where(block_mask[:, None, :, None], shaped, jnp.zeros((), weight.dtype))
    return masked.reshape(weight.shape)


def row_perm(n_row, step):
    n_y = n_row // 2
    return [(y * 2 + c, ((y + step) % n_y) * 2 + c) for y in range(n_y) for c in range(2)]


def row_reduce_scatter(tokens, weights, n_row, after):
    n_y = n_row // 2
    r = lax.axis_index("row")
    y = r // 2
    core = r % 2
    rows = tokens.shape[0]
    width = weights.shape[1]
    halves = tokens.reshape(2, rows // 2, tokens.shape[1])
    send = lax.dynamic_index_in_dim(halves, 1 - core, 0, keepdims=False)
    keep = lax.dynamic_index_in_dim(halves, core, 0, keepdims=False)
    send = jnp.dot(send, weights, preferred_element_type=jnp.float32).astype(jnp.bfloat16)
    swap = [(i, i ^ 1) for i in range(n_row)]
    got = lax.ppermute(send, "row", swap)
    keep = jnp.dot(keep, weights, preferred_element_type=jnp.float32).astype(jnp.bfloat16)
    pair = (keep.astype(jnp.float32) + got.astype(jnp.float32)).astype(jnp.bfloat16)
    if after is not None:
        pair, after = lax.optimization_barrier((pair, after))
    chunk = rows // 2 // n_y
    pair = pair.reshape(n_y, chunk, width)
    results = []
    for direction, cols in ((1, slice(0, width // 2)), (-1, slice(width // 2, width))):
        own = pair[:, :, cols]
        index = (y - direction) % n_y
        acc = lax.dynamic_index_in_dim(own, index, 0, keepdims=False)
        for step in range(n_y - 1):
            got = lax.ppermute(acc.astype(jnp.bfloat16), "row", row_perm(n_row, direction))
            index = (index - direction) % n_y
            acc = got.astype(jnp.float32) + lax.dynamic_index_in_dim(own, index, 0, keepdims=False)
        results.append(acc)
    return results


def row_all_gather(value, n_row):
    n_y = n_row // 2
    r = lax.axis_index("row")
    y = r // 2
    core = r % 2
    chunk, width = value.shape
    parts = []
    for direction, cols in ((1, slice(0, width // 2)), (-1, slice(width // 2, width))):
        held = value[:, cols]
        full = jnp.zeros((n_y, chunk, width // 2), value.dtype)
        full = lax.dynamic_update_index_in_dim(full, held, y, 0)
        for step in range(n_y - 1):
            held = lax.ppermute(held, "row", row_perm(n_row, direction))
            full = lax.dynamic_update_index_in_dim(full, held, (y - direction * (step + 1)) % n_y, 0)
        parts.append(full)
    half = jnp.concatenate(parts, axis=2).reshape(n_y * chunk, width)
    swap = [(i, i ^ 1) for i in range(n_row)]
    other = lax.ppermute(half, "row", swap)
    both = jnp.zeros((2, n_y * chunk, width), value.dtype)
    both = lax.dynamic_update_index_in_dim(both, half, core, 0)
    both = lax.dynamic_update_index_in_dim(both, other, 1 - core, 0)
    return both.reshape(2 * n_y * chunk, width)


def ring_reduce_scatter(own, pos, n, perm_of):
    width = own.shape[2]
    halves = []
    for direction, cols in ((1, slice(0, width // 2)), (-1, slice(width // 2, width))):
        part = own[:, :, cols]
        index = (pos - direction) % n
        acc = lax.dynamic_index_in_dim(part, index, 0, keepdims=False).astype(jnp.float32)
        for step in range(n - 1):
            got = lax.ppermute(acc.astype(jnp.bfloat16), "col", perm_of(direction))
            index = (index - direction) % n
            acc = got.astype(jnp.float32) + lax.dynamic_index_in_dim(part, index, 0, keepdims=False)
        halves.append(acc)
    return jnp.concatenate(halves, axis=1)


def ring_all_gather(value, pos, n, perm_of):
    chunk, width = value.shape
    parts = []
    for direction, cols in ((1, slice(0, width // 2)), (-1, slice(width // 2, width))):
        held = value[:, cols]
        full = jnp.zeros((n, chunk, width // 2), value.dtype)
        full = lax.dynamic_update_index_in_dim(full, held, pos, 0)
        for step in range(n - 1):
            held = lax.ppermute(held, "col", perm_of(direction))
            full = lax.dynamic_update_index_in_dim(full, held, (pos - direction * (step + 1)) % n, 0)
        parts.append(full)
    return jnp.concatenate(parts, axis=2)


def col_axes(n_col):
    n_z = 4 if n_col % 4 == 0 else 1
    n_x = n_col // n_z
    c = lax.axis_index("col")

    def x_perm(d):
        return [(i * n_z + j, ((i + d) % n_x) * n_z + j) for i in range(n_x) for j in range(n_z)]

    def z_perm(d):
        return [(i * n_z + j, i * n_z + (j + d) % n_z) for i in range(n_x) for j in range(n_z)]

    return n_x, n_z, c // n_z, c % n_z, x_perm, z_perm


def col_all_gather(value, n_col):
    n_x, n_z, x, z, x_perm, z_perm = col_axes(n_col)
    rows, width = value.shape
    part = ring_all_gather(value, z, n_z, z_perm).reshape(n_z * rows, width)
    return ring_all_gather(part, x, n_x, x_perm).reshape(n_x * n_z * rows, width)


def col_reduce_scatter(terms, n_col):
    n_z = 4 if n_col % 4 == 0 else 1
    n_x = n_col // n_z
    c = lax.axis_index("col")
    x = c // n_z
    z = c % n_z
    rows, width = terms.shape

    def x_perm(d):
        return [(i * n_z + j, ((i + d) % n_x) * n_z + j) for i in range(n_x) for j in range(n_z)]

    def z_perm(d):
        return [(i * n_z + j, i * n_z + (j + d) % n_z) for i in range(n_x) for j in range(n_z)]

    part = ring_reduce_scatter(terms.reshape(n_x, rows // n_x, width), x, n_x, x_perm)
    part = part.astype(jnp.bfloat16).reshape(n_z, rows // n_x // n_z, width)
    return ring_reduce_scatter(part, z, n_z, z_perm).astype(jnp.bfloat16)


def on_device(
    tokens,
    gate_weight,
    up_weight,
    down_weight,
    gate_keep,
    gate_count,
    up_keep,
    up_count,
    down_keep,
    down_count,
):
    model_blocks = gate_weight.shape[0] // BLOCK
    hidden_blocks = gate_weight.shape[1] // BLOCK
    n_col = lax.axis_size("col")
    n_row = lax.axis_size("row")
    row_offset = lax.axis_index("row") * model_blocks
    col_offset = lax.axis_index("col") * hidden_blocks
    gate_pruned = apply_mask(
        gate_weight, local_mask(gate_keep, gate_count, row_offset, model_blocks).T, BLOCK
    )
    up_pruned = apply_mask(
        up_weight, local_mask(up_keep, up_count, row_offset, model_blocks).T, BLOCK
    )
    down_pruned = apply_mask(
        down_weight, local_mask(down_keep, down_count, col_offset, hidden_blocks).T, BLOCK
    )
    both_weights = jnp.concatenate([gate_pruned, up_pruned], axis=1)
    rows = tokens.shape[0] // CHUNKS
    gathered = lax.all_gather(tokens, "col", axis=0, tiled=True)
    gathered = gathered.reshape(n_col, CHUNKS, rows, gathered.shape[1])
    outs = []
    previous = None
    for k in range(CHUNKS):
        chunk = gathered[:, k].reshape(n_col * rows, gathered.shape[3])
        gate_sums, up_sums = row_reduce_scatter(chunk, both_weights, n_row, previous)
        hidden = (jax.nn.silu(gate_sums) * up_sums).astype(jnp.bfloat16)
        hidden = row_all_gather(hidden, n_row)
        terms = jnp.dot(hidden, down_pruned, preferred_element_type=jnp.float32).astype(
            jnp.bfloat16
        )
        previous = terms
        if COL_RING:
            outs.append(col_reduce_scatter(terms, n_col))
        elif COL_A2A and k == CHUNKS - 1:
            split = terms.shape[1] // 2
            left = lax.psum_scatter(terms[:, :split], "col", scatter_dimension=0, tiled=True)
            right = terms[:, split:].reshape(n_col, rows, terms.shape[1] - split)
            right = lax.all_to_all(right, "col", 0, 0, tiled=False)
            right = jnp.sum(right.astype(jnp.float32), axis=0).astype(jnp.bfloat16)
            outs.append(jnp.concatenate([left, right], axis=1))
        else:
            outs.append(lax.psum_scatter(terms, "col", scatter_dimension=0, tiled=True))
    return jnp.concatenate(outs, axis=0)


def solution(mesh):
    return jax.shard_map(
        on_device,
        mesh=mesh,
        in_specs=(
            P("col", "row"),
            P("row", "col"),
            P("row", "col"),
            P("col", "row"),
            P("col", None),
            P("col"),
            P("col", None),
            P("col"),
            P("row", None),
            P("row"),
        ),
        out_specs=P("col", "row"),
        check_vma=False,
    )
```

```python
import jax
import jax.numpy as jnp
from jax import lax
from jax.sharding import PartitionSpec as P

BLOCK = 128
CHUNKS = 1
COL_A2A = True
COL_RING = False


def local_mask(keep_list, keep_count, offset, blocks):
    position = jnp.arange(keep_list.shape[1], dtype=jnp.int32)
    active_slot = position[None, :] < keep_count[:, None]
    local_index = keep_list - offset
    matches = (
        local_index[:, :, None] == jnp.arange(blocks, dtype=jnp.int32)[None, None, :]
    ) & active_slot[:, :, None]
    return jnp.any(matches, axis=1)


def apply_mask(weight, block_mask, block_size):
    block_rows, block_cols = block_mask.shape
    shaped = weight.reshape(block_rows, block_size, block_cols, block_size)
    masked = jnp.where(block_mask[:, None, :, None], shaped, jnp.zeros((), weight.dtype))
    return masked.reshape(weight.shape)


def row_perm(n_row, step):
    n_y = n_row // 2
    return [(y * 2 + c, ((y + step) % n_y) * 2 + c) for y in range(n_y) for c in range(2)]


def row_reduce_scatter(tokens, weights, n_row, after):
    n_y = n_row // 2
    r = lax.axis_index("row")
    y = r // 2
    core = r % 2
    rows = tokens.shape[0]
    width = weights.shape[1]
    halves = tokens.reshape(2, rows // 2, tokens.shape[1])
    send = lax.dynamic_index_in_dim(halves, 1 - core, 0, keepdims=False)
    keep = lax.dynamic_index_in_dim(halves, core, 0, keepdims=False)
    send = jnp.dot(send, weights, preferred_element_type=jnp.float32).astype(jnp.bfloat16)
    swap = [(i, i ^ 1) for i in range(n_row)]
    got = lax.ppermute(send, "row", swap)
    keep = jnp.dot(keep, weights, preferred_element_type=jnp.float32).astype(jnp.bfloat16)
    keep = lax.optimization_barrier(keep)
    pair = (keep.astype(jnp.float32) + got.astype(jnp.float32)).astype(jnp.bfloat16)
    if after is not None:
        pair, after = lax.optimization_barrier((pair, after))
    chunk = rows // 2 // n_y
    pair = pair.reshape(n_y, chunk, width)
    results = []
    for direction, cols in ((1, slice(0, width // 2)), (-1, slice(width // 2, width))):
        own = pair[:, :, cols]
        index = (y - direction) % n_y
        acc = lax.dynamic_index_in_dim(own, index, 0, keepdims=False)
        for step in range(n_y - 1):
            got = lax.ppermute(acc.astype(jnp.bfloat16), "row", row_perm(n_row, direction))
            index = (index - direction) % n_y
            acc = got.astype(jnp.float32) + lax.dynamic_index_in_dim(own, index, 0, keepdims=False)
        results.append(acc)
    return results


def row_all_gather(value, n_row, down):
    n_y = n_row // 2
    r = lax.axis_index("row")
    y = r // 2
    core = r % 2
    chunk, width = value.shape
    parts = []
    for direction, cols in ((1, slice(0, width // 2)), (-1, slice(width // 2, width))):
        held = value[:, cols]
        full = jnp.zeros((n_y, chunk, width // 2), value.dtype)
        full = lax.dynamic_update_index_in_dim(full, held, y, 0)
        for step in range(n_y - 1):
            held = lax.ppermute(held, "row", row_perm(n_row, direction))
            full = lax.dynamic_update_index_in_dim(full, held, (y - direction * (step + 1)) % n_y, 0)
        parts.append(full)
    half = jnp.concatenate(parts, axis=2).reshape(n_y * chunk, width)
    swap = [(i, i ^ 1) for i in range(n_row)]
    other = lax.ppermute(half, "row", swap)
    mine = jnp.dot(half, down, preferred_element_type=jnp.float32).astype(jnp.bfloat16)
    theirs = jnp.dot(other, down, preferred_element_type=jnp.float32).astype(jnp.bfloat16)
    both = jnp.zeros((2, n_y * chunk, down.shape[1]), jnp.bfloat16)
    both = lax.dynamic_update_index_in_dim(both, mine, core, 0)
    both = lax.dynamic_update_index_in_dim(both, theirs, 1 - core, 0)
    return both.reshape(2 * n_y * chunk, down.shape[1])


def ring_reduce_scatter(own, pos, n, perm_of):
    width = own.shape[2]
    halves = []
    for direction, cols in ((1, slice(0, width // 2)), (-1, slice(width // 2, width))):
        part = own[:, :, cols]
        index = (pos - direction) % n
        acc = lax.dynamic_index_in_dim(part, index, 0, keepdims=False).astype(jnp.float32)
        for step in range(n - 1):
            got = lax.ppermute(acc.astype(jnp.bfloat16), "col", perm_of(direction))
            index = (index - direction) % n
            acc = got.astype(jnp.float32) + lax.dynamic_index_in_dim(part, index, 0, keepdims=False)
        halves.append(acc)
    return jnp.concatenate(halves, axis=1)


def ring_all_gather(value, pos, n, perm_of):
    chunk, width = value.shape
    parts = []
    for direction, cols in ((1, slice(0, width // 2)), (-1, slice(width // 2, width))):
        held = value[:, cols]
        full = jnp.zeros((n, chunk, width // 2), value.dtype)
        full = lax.dynamic_update_index_in_dim(full, held, pos, 0)
        for step in range(n - 1):
            held = lax.ppermute(held, "col", perm_of(direction))
            full = lax.dynamic_update_index_in_dim(full, held, (pos - direction * (step + 1)) % n, 0)
        parts.append(full)
    return jnp.concatenate(parts, axis=2)


def col_axes(n_col):
    n_z = 4 if n_col % 4 == 0 else 1
    n_x = n_col // n_z
    c = lax.axis_index("col")

    def x_perm(d):
        return [(i * n_z + j, ((i + d) % n_x) * n_z + j) for i in range(n_x) for j in range(n_z)]

    def z_perm(d):
        return [(i * n_z + j, i * n_z + (j + d) % n_z) for i in range(n_x) for j in range(n_z)]

    return n_x, n_z, c // n_z, c % n_z, x_perm, z_perm


def col_all_gather(value, n_col):
    n_x, n_z, x, z, x_perm, z_perm = col_axes(n_col)
    rows, width = value.shape
    part = ring_all_gather(value, z, n_z, z_perm).reshape(n_z * rows, width)
    return ring_all_gather(part, x, n_x, x_perm).reshape(n_x * n_z * rows, width)


def col_reduce_scatter(terms, n_col):
    n_z = 4 if n_col % 4 == 0 else 1
    n_x = n_col // n_z
    c = lax.axis_index("col")
    x = c // n_z
    z = c % n_z
    rows, width = terms.shape

    def x_perm(d):
        return [(i * n_z + j, ((i + d) % n_x) * n_z + j) for i in range(n_x) for j in range(n_z)]

    def z_perm(d):
        return [(i * n_z + j, i * n_z + (j + d) % n_z) for i in range(n_x) for j in range(n_z)]

    part = ring_reduce_scatter(terms.reshape(n_x, rows // n_x, width), x, n_x, x_perm)
    part = part.astype(jnp.bfloat16).reshape(n_z, rows // n_x // n_z, width)
    return ring_reduce_scatter(part, z, n_z, z_perm).astype(jnp.bfloat16)


def on_device(
    tokens,
    gate_weight,
    up_weight,
    down_weight,
    gate_keep,
    gate_count,
    up_keep,
    up_count,
    down_keep,
    down_count,
):
    model_blocks = gate_weight.shape[0] // BLOCK
    hidden_blocks = gate_weight.shape[1] // BLOCK
    n_col = lax.axis_size("col")
    n_row = lax.axis_size("row")
    row_offset = lax.axis_index("row") * model_blocks
    col_offset = lax.axis_index("col") * hidden_blocks
    gate_pruned = apply_mask(
        gate_weight, local_mask(gate_keep, gate_count, row_offset, model_blocks).T, BLOCK
    )
    up_pruned = apply_mask(
        up_weight, local_mask(up_keep, up_count, row_offset, model_blocks).T, BLOCK
    )
    down_pruned = apply_mask(
        down_weight, local_mask(down_keep, down_count, col_offset, hidden_blocks).T, BLOCK
    )
    both_weights = jnp.concatenate([gate_pruned, up_pruned], axis=1)
    rows = tokens.shape[0] // CHUNKS
    gathered = lax.all_gather(tokens, "col", axis=0, tiled=True)
    gathered = gathered.reshape(n_col, CHUNKS, rows, gathered.shape[1])
    outs = []
    previous = None
    for k in range(CHUNKS):
        chunk = gathered[:, k].reshape(n_col * rows, gathered.shape[3])
        gate_sums, up_sums = row_reduce_scatter(chunk, both_weights, n_row, previous)
        hidden = (jax.nn.silu(gate_sums) * up_sums).astype(jnp.bfloat16)
        terms = row_all_gather(hidden, n_row, down_pruned)
        previous = terms
        if COL_RING:
            outs.append(col_reduce_scatter(terms, n_col))
        elif COL_A2A and k == CHUNKS - 1:
            terms = terms.reshape(n_col, rows, terms.shape[1])
            terms = lax.all_to_all(terms, "col", 0, 0, tiled=False)
            outs.append(jnp.sum(terms.astype(jnp.float32), axis=0).astype(jnp.bfloat16))
        else:
            outs.append(lax.psum_scatter(terms, "col", scatter_dimension=0, tiled=True))
    return jnp.concatenate(outs, axis=0)


def solution(mesh):
    return jax.shard_map(
        on_device,
        mesh=mesh,
        in_specs=(
            P("col", "row"),
            P("row", "col"),
            P("row", "col"),
            P("col", "row"),
            P("col", None),
            P("col"),
            P("col", None),
            P("col"),
            P("row", None),
            P("row"),
        ),
        out_specs=P("col", "row"),
        check_vma=False,
    )
```

```python
import jax
import jax.numpy as jnp
from jax import lax
from jax.sharding import PartitionSpec as P

BLOCK = 128
CHUNKS = 1
COL_A2A = True
COL_RING = False


def local_mask(keep_list, keep_count, offset, blocks):
    position = jnp.arange(keep_list.shape[1], dtype=jnp.int32)
    active_slot = position[None, :] < keep_count[:, None]
    local_index = keep_list - offset
    matches = (
        local_index[:, :, None] == jnp.arange(blocks, dtype=jnp.int32)[None, None, :]
    ) & active_slot[:, :, None]
    return jnp.any(matches, axis=1)


def apply_mask(weight, block_mask, block_size):
    block_rows, block_cols = block_mask.shape
    shaped = weight.reshape(block_rows, block_size, block_cols, block_size)
    masked = jnp.where(block_mask[:, None, :, None], shaped, jnp.zeros((), weight.dtype))
    return masked.reshape(weight.shape)


def row_perm(n_row, step):
    n_y = n_row // 2
    return [(y * 2 + c, ((y + step) % n_y) * 2 + c) for y in range(n_y) for c in range(2)]


def row_reduce_scatter(tokens, weights, n_row, after):
    n_y = n_row // 2
    r = lax.axis_index("row")
    y = r // 2
    core = r % 2
    rows = tokens.shape[0]
    width = weights.shape[1]
    halves = tokens.reshape(2, rows // 2, tokens.shape[1])
    send = lax.dynamic_index_in_dim(halves, 1 - core, 0, keepdims=False)
    keep = lax.dynamic_index_in_dim(halves, core, 0, keepdims=False)
    send = jnp.dot(send, weights, preferred_element_type=jnp.float32).astype(jnp.bfloat16)
    swap = [(i, i ^ 1) for i in range(n_row)]
    got = lax.ppermute(send, "row", swap)
    keep = jnp.dot(keep, weights, preferred_element_type=jnp.float32).astype(jnp.bfloat16)
    keep = lax.optimization_barrier(keep)
    if after is not None:
        keep, got, after = lax.optimization_barrier((keep, got, after))
    chunk = rows // 2 // n_y
    keep = keep.reshape(n_y, chunk, width)
    got = got.reshape(n_y, chunk, width)
    results = []
    for direction, cols in ((1, slice(0, width // 2)), (-1, slice(width // 2, width))):

        def own(index, cols=cols):
            mine = lax.dynamic_index_in_dim(keep, index, 0, keepdims=False)[:, cols]
            theirs = lax.dynamic_index_in_dim(got, index, 0, keepdims=False)[:, cols]
            return mine.astype(jnp.float32) + theirs.astype(jnp.float32)

        index = (y - direction) % n_y
        acc = own(index)
        for step in range(n_y - 1):
            received = lax.ppermute(acc.astype(jnp.bfloat16), "row", row_perm(n_row, direction))
            index = (index - direction) % n_y
            acc = received.astype(jnp.float32) + own(index)
        results.append(acc)
    return results


def row_all_gather(value, n_row, down):
    n_y = n_row // 2
    r = lax.axis_index("row")
    y = r // 2
    core = r % 2
    chunk, width = value.shape
    parts = []
    for direction, cols in ((1, slice(0, width // 2)), (-1, slice(width // 2, width))):
        held = value[:, cols]
        full = jnp.zeros((n_y, chunk, width // 2), value.dtype)
        full = lax.dynamic_update_index_in_dim(full, held, y, 0)
        for step in range(n_y - 1):
            held = lax.ppermute(held, "row", row_perm(n_row, direction))
            full = lax.dynamic_update_index_in_dim(full, held, (y - direction * (step + 1)) % n_y, 0)
        parts.append(full)
    half = jnp.concatenate(parts, axis=2).reshape(n_y * chunk, width)
    swap = [(i, i ^ 1) for i in range(n_row)]
    other = lax.ppermute(half, "row", swap)
    mine = jnp.dot(half, down, preferred_element_type=jnp.float32).astype(jnp.bfloat16)
    theirs = jnp.dot(other, down, preferred_element_type=jnp.float32).astype(jnp.bfloat16)
    both = jnp.zeros((2, n_y * chunk, down.shape[1]), jnp.bfloat16)
    both = lax.dynamic_update_index_in_dim(both, mine, core, 0)
    both = lax.dynamic_update_index_in_dim(both, theirs, 1 - core, 0)
    return both.reshape(2 * n_y * chunk, down.shape[1])


def ring_reduce_scatter(own, pos, n, perm_of):
    width = own.shape[2]
    halves = []
    for direction, cols in ((1, slice(0, width // 2)), (-1, slice(width // 2, width))):
        part = own[:, :, cols]
        index = (pos - direction) % n
        acc = lax.dynamic_index_in_dim(part, index, 0, keepdims=False).astype(jnp.float32)
        for step in range(n - 1):
            got = lax.ppermute(acc.astype(jnp.bfloat16), "col", perm_of(direction))
            index = (index - direction) % n
            acc = got.astype(jnp.float32) + lax.dynamic_index_in_dim(part, index, 0, keepdims=False)
        halves.append(acc)
    return jnp.concatenate(halves, axis=1)


def ring_all_gather(value, pos, n, perm_of):
    chunk, width = value.shape
    parts = []
    for direction, cols in ((1, slice(0, width // 2)), (-1, slice(width // 2, width))):
        held = value[:, cols]
        full = jnp.zeros((n, chunk, width // 2), value.dtype)
        full = lax.dynamic_update_index_in_dim(full, held, pos, 0)
        for step in range(n - 1):
            held = lax.ppermute(held, "col", perm_of(direction))
            full = lax.dynamic_update_index_in_dim(full, held, (pos - direction * (step + 1)) % n, 0)
        parts.append(full)
    return jnp.concatenate(parts, axis=2)


def col_axes(n_col):
    n_z = 4 if n_col % 4 == 0 else 1
    n_x = n_col // n_z
    c = lax.axis_index("col")

    def x_perm(d):
        return [(i * n_z + j, ((i + d) % n_x) * n_z + j) for i in range(n_x) for j in range(n_z)]

    def z_perm(d):
        return [(i * n_z + j, i * n_z + (j + d) % n_z) for i in range(n_x) for j in range(n_z)]

    return n_x, n_z, c // n_z, c % n_z, x_perm, z_perm


def col_all_gather(value, n_col):
    n_x, n_z, x, z, x_perm, z_perm = col_axes(n_col)
    rows, width = value.shape
    part = ring_all_gather(value, z, n_z, z_perm).reshape(n_z * rows, width)
    return ring_all_gather(part, x, n_x, x_perm).reshape(n_x * n_z * rows, width)


def col_reduce_scatter(terms, n_col):
    n_z = 4 if n_col % 4 == 0 else 1
    n_x = n_col // n_z
    c = lax.axis_index("col")
    x = c // n_z
    z = c % n_z
    rows, width = terms.shape

    def x_perm(d):
        return [(i * n_z + j, ((i + d) % n_x) * n_z + j) for i in range(n_x) for j in range(n_z)]

    def z_perm(d):
        return [(i * n_z + j, i * n_z + (j + d) % n_z) for i in range(n_x) for j in range(n_z)]

    part = ring_reduce_scatter(terms.reshape(n_x, rows // n_x, width), x, n_x, x_perm)
    part = part.astype(jnp.bfloat16).reshape(n_z, rows // n_x // n_z, width)
    return ring_reduce_scatter(part, z, n_z, z_perm).astype(jnp.bfloat16)


def on_device(
    tokens,
    gate_weight,
    up_weight,
    down_weight,
    gate_keep,
    gate_count,
    up_keep,
    up_count,
    down_keep,
    down_count,
):
    model_blocks = gate_weight.shape[0] // BLOCK
    hidden_blocks = gate_weight.shape[1] // BLOCK
    n_col = lax.axis_size("col")
    n_row = lax.axis_size("row")
    row_offset = lax.axis_index("row") * model_blocks
    col_offset = lax.axis_index("col") * hidden_blocks
    gate_pruned = apply_mask(
        gate_weight, local_mask(gate_keep, gate_count, row_offset, model_blocks).T, BLOCK
    )
    up_pruned = apply_mask(
        up_weight, local_mask(up_keep, up_count, row_offset, model_blocks).T, BLOCK
    )
    down_pruned = apply_mask(
        down_weight, local_mask(down_keep, down_count, col_offset, hidden_blocks).T, BLOCK
    )
    both_weights = jnp.concatenate([gate_pruned, up_pruned], axis=1)
    rows = tokens.shape[0] // CHUNKS
    gathered = lax.all_gather(tokens, "col", axis=0, tiled=True)
    gathered = gathered.reshape(n_col, CHUNKS, rows, gathered.shape[1])
    outs = []
    previous = None
    for k in range(CHUNKS):
        chunk = gathered[:, k].reshape(n_col * rows, gathered.shape[3])
        gate_sums, up_sums = row_reduce_scatter(chunk, both_weights, n_row, previous)
        hidden = (jax.nn.silu(gate_sums) * up_sums).astype(jnp.bfloat16)
        terms = row_all_gather(hidden, n_row, down_pruned)
        previous = terms
        if COL_RING:
            outs.append(col_reduce_scatter(terms, n_col))
        elif COL_A2A and k == CHUNKS - 1:
            terms = terms.reshape(n_col, rows, terms.shape[1])
            terms = lax.all_to_all(terms, "col", 0, 0, tiled=False)
            outs.append(jnp.sum(terms.astype(jnp.float32), axis=0).astype(jnp.bfloat16))
        else:
            outs.append(lax.psum_scatter(terms, "col", scatter_dimension=0, tiled=True))
    return jnp.concatenate(outs, axis=0)


def solution(mesh):
    return jax.shard_map(
        on_device,
        mesh=mesh,
        in_specs=(
            P("col", "row"),
            P("row", "col"),
            P("row", "col"),
            P("col", "row"),
            P("col", None),
            P("col"),
            P("col", None),
            P("col"),
            P("row", None),
            P("row"),
        ),
        out_specs=P("col", "row"),
        check_vma=False,
    )
```

```python
import jax
import jax.numpy as jnp
from jax import lax
from jax.sharding import PartitionSpec as P

BLOCK = 128
CHUNKS = 1
COL_A2A = True
COL_RING = False


def local_mask(keep_list, keep_count, offset, blocks):
    position = jnp.arange(keep_list.shape[1], dtype=jnp.int32)
    active_slot = position[None, :] < keep_count[:, None]
    local_index = keep_list - offset
    matches = (
        local_index[:, :, None] == jnp.arange(blocks, dtype=jnp.int32)[None, None, :]
    ) & active_slot[:, :, None]
    return jnp.any(matches, axis=1)


def apply_mask(weight, block_mask, block_size):
    block_rows, block_cols = block_mask.shape
    shaped = weight.reshape(block_rows, block_size, block_cols, block_size)
    masked = jnp.where(block_mask[:, None, :, None], shaped, jnp.zeros((), weight.dtype))
    return masked.reshape(weight.shape)


def row_perm(n_row, step):
    n_y = n_row // 2
    return [(y * 2 + c, ((y + step) % n_y) * 2 + c) for y in range(n_y) for c in range(2)]


def row_reduce_scatter(tokens, weights, n_row, after):
    n_y = n_row // 2
    r = lax.axis_index("row")
    y = r // 2
    core = r % 2
    rows = tokens.shape[0]
    halves = tokens.reshape(2, rows // 2, tokens.shape[1])
    send = lax.dynamic_index_in_dim(halves, 1 - core, 0, keepdims=False)
    keep = lax.dynamic_index_in_dim(halves, core, 0, keepdims=False)
    swap = [(i, i ^ 1) for i in range(n_row)]
    chunk = rows // 2 // n_y
    sent = []
    for w in weights:
        part = jnp.dot(send, w, preferred_element_type=jnp.float32).astype(jnp.bfloat16)
        sent.append(lax.ppermute(part, "row", swap))
    results = []
    for direction, w, got in ((1, weights[0], sent[0]), (-1, weights[1], sent[1])):
        mine = jnp.dot(keep, w, preferred_element_type=jnp.float32).astype(jnp.bfloat16)
        mine = lax.optimization_barrier(mine).reshape(n_y, chunk, w.shape[1])
        got = got.reshape(n_y, chunk, w.shape[1])

        def own(index, mine=mine, got=got):
            return (
                lax.dynamic_index_in_dim(mine, index, 0, keepdims=False).astype(jnp.float32)
                + lax.dynamic_index_in_dim(got, index, 0, keepdims=False).astype(jnp.float32)
            )

        index = (y - direction) % n_y
        acc = own(index)
        for step in range(n_y - 1):
            received = lax.ppermute(acc.astype(jnp.bfloat16), "row", row_perm(n_row, direction))
            index = (index - direction) % n_y
            acc = received.astype(jnp.float32) + own(index)
        results.append(acc)
    return results


def row_all_gather(value, n_row, down):
    n_y = n_row // 2
    r = lax.axis_index("row")
    y = r // 2
    core = r % 2
    chunk, width = value.shape
    parts = []
    for direction, cols in ((1, slice(0, width // 2)), (-1, slice(width // 2, width))):
        held = value[:, cols]
        full = jnp.zeros((n_y, chunk, width // 2), value.dtype)
        full = lax.dynamic_update_index_in_dim(full, held, y, 0)
        for step in range(n_y - 1):
            held = lax.ppermute(held, "row", row_perm(n_row, direction))
            full = lax.dynamic_update_index_in_dim(full, held, (y - direction * (step + 1)) % n_y, 0)
        parts.append(full)
    half = jnp.concatenate(parts, axis=2).reshape(n_y * chunk, width)
    swap = [(i, i ^ 1) for i in range(n_row)]
    other = lax.ppermute(half, "row", swap)
    mine = jnp.dot(half, down, preferred_element_type=jnp.float32).astype(jnp.bfloat16)
    theirs = jnp.dot(other, down, preferred_element_type=jnp.float32).astype(jnp.bfloat16)
    both = jnp.zeros((2, n_y * chunk, down.shape[1]), jnp.bfloat16)
    both = lax.dynamic_update_index_in_dim(both, mine, core, 0)
    both = lax.dynamic_update_index_in_dim(both, theirs, 1 - core, 0)
    return both.reshape(2 * n_y * chunk, down.shape[1])


def ring_reduce_scatter(own, pos, n, perm_of):
    width = own.shape[2]
    halves = []
    for direction, cols in ((1, slice(0, width // 2)), (-1, slice(width // 2, width))):
        part = own[:, :, cols]
        index = (pos - direction) % n
        acc = lax.dynamic_index_in_dim(part, index, 0, keepdims=False).astype(jnp.float32)
        for step in range(n - 1):
            got = lax.ppermute(acc.astype(jnp.bfloat16), "col", perm_of(direction))
            index = (index - direction) % n
            acc = got.astype(jnp.float32) + lax.dynamic_index_in_dim(part, index, 0, keepdims=False)
        halves.append(acc)
    return jnp.concatenate(halves, axis=1)


def ring_all_gather(value, pos, n, perm_of):
    chunk, width = value.shape
    parts = []
    for direction, cols in ((1, slice(0, width // 2)), (-1, slice(width // 2, width))):
        held = value[:, cols]
        full = jnp.zeros((n, chunk, width // 2), value.dtype)
        full = lax.dynamic_update_index_in_dim(full, held, pos, 0)
        for step in range(n - 1):
            held = lax.ppermute(held, "col", perm_of(direction))
            full = lax.dynamic_update_index_in_dim(full, held, (pos - direction * (step + 1)) % n, 0)
        parts.append(full)
    return jnp.concatenate(parts, axis=2)


def col_axes(n_col):
    n_z = 4 if n_col % 4 == 0 else 1
    n_x = n_col // n_z
    c = lax.axis_index("col")

    def x_perm(d):
        return [(i * n_z + j, ((i + d) % n_x) * n_z + j) for i in range(n_x) for j in range(n_z)]

    def z_perm(d):
        return [(i * n_z + j, i * n_z + (j + d) % n_z) for i in range(n_x) for j in range(n_z)]

    return n_x, n_z, c // n_z, c % n_z, x_perm, z_perm


def col_all_gather(value, n_col):
    n_x, n_z, x, z, x_perm, z_perm = col_axes(n_col)
    rows, width = value.shape
    part = ring_all_gather(value, z, n_z, z_perm).reshape(n_z * rows, width)
    return ring_all_gather(part, x, n_x, x_perm).reshape(n_x * n_z * rows, width)


def col_reduce_scatter(terms, n_col):
    n_z = 4 if n_col % 4 == 0 else 1
    n_x = n_col // n_z
    c = lax.axis_index("col")
    x = c // n_z
    z = c % n_z
    rows, width = terms.shape

    def x_perm(d):
        return [(i * n_z + j, ((i + d) % n_x) * n_z + j) for i in range(n_x) for j in range(n_z)]

    def z_perm(d):
        return [(i * n_z + j, i * n_z + (j + d) % n_z) for i in range(n_x) for j in range(n_z)]

    part = ring_reduce_scatter(terms.reshape(n_x, rows // n_x, width), x, n_x, x_perm)
    part = part.astype(jnp.bfloat16).reshape(n_z, rows // n_x // n_z, width)
    return ring_reduce_scatter(part, z, n_z, z_perm).astype(jnp.bfloat16)


def on_device(
    tokens,
    gate_weight,
    up_weight,
    down_weight,
    gate_keep,
    gate_count,
    up_keep,
    up_count,
    down_keep,
    down_count,
):
    model_blocks = gate_weight.shape[0] // BLOCK
    hidden_blocks = gate_weight.shape[1] // BLOCK
    n_col = lax.axis_size("col")
    n_row = lax.axis_size("row")
    row_offset = lax.axis_index("row") * model_blocks
    col_offset = lax.axis_index("col") * hidden_blocks
    gate_pruned = apply_mask(
        gate_weight, local_mask(gate_keep, gate_count, row_offset, model_blocks).T, BLOCK
    )
    up_pruned = apply_mask(
        up_weight, local_mask(up_keep, up_count, row_offset, model_blocks).T, BLOCK
    )
    down_pruned = apply_mask(
        down_weight, local_mask(down_keep, down_count, col_offset, hidden_blocks).T, BLOCK
    )
    rows = tokens.shape[0] // CHUNKS
    gathered = lax.all_gather(tokens, "col", axis=0, tiled=True)
    gathered = gathered.reshape(n_col, CHUNKS, rows, gathered.shape[1])
    outs = []
    previous = None
    for k in range(CHUNKS):
        chunk = gathered[:, k].reshape(n_col * rows, gathered.shape[3])
        gate_sums, up_sums = row_reduce_scatter(chunk, (gate_pruned, up_pruned), n_row, previous)
        hidden = (jax.nn.silu(gate_sums) * up_sums).astype(jnp.bfloat16)
        terms = row_all_gather(hidden, n_row, down_pruned)
        previous = terms
        if COL_RING:
            outs.append(col_reduce_scatter(terms, n_col))
        elif COL_A2A and k == CHUNKS - 1:
            terms = terms.reshape(n_col, rows, terms.shape[1])
            terms = lax.all_to_all(terms, "col", 0, 0, tiled=False)
            outs.append(jnp.sum(terms.astype(jnp.float32), axis=0).astype(jnp.bfloat16))
        else:
            outs.append(lax.psum_scatter(terms, "col", scatter_dimension=0, tiled=True))
    return jnp.concatenate(outs, axis=0)


def solution(mesh):
    return jax.shard_map(
        on_device,
        mesh=mesh,
        in_specs=(
            P("col", "row"),
            P("row", "col"),
            P("row", "col"),
            P("col", "row"),
            P("col", None),
            P("col"),
            P("col", None),
            P("col"),
            P("row", None),
            P("row"),
        ),
        out_specs=P("col", "row"),
        check_vma=False,
    )
```

```python
import jax
import jax.numpy as jnp
from jax import lax
from jax.sharding import PartitionSpec as P

BLOCK = 128
CHUNKS = 1
COL_A2A = True
COL_RING = False
SUB_RINGS = 2


def local_mask(keep_list, keep_count, offset, blocks):
    position = jnp.arange(keep_list.shape[1], dtype=jnp.int32)
    active_slot = position[None, :] < keep_count[:, None]
    local_index = keep_list - offset
    matches = (
        local_index[:, :, None] == jnp.arange(blocks, dtype=jnp.int32)[None, None, :]
    ) & active_slot[:, :, None]
    return jnp.any(matches, axis=1)


def apply_mask(weight, block_mask, block_size):
    block_rows, block_cols = block_mask.shape
    shaped = weight.reshape(block_rows, block_size, block_cols, block_size)
    masked = jnp.where(block_mask[:, None, :, None], shaped, jnp.zeros((), weight.dtype))
    return masked.reshape(weight.shape)


def row_perm(n_row, step):
    n_y = n_row // 2
    return [(y * 2 + c, ((y + step) % n_y) * 2 + c) for y in range(n_y) for c in range(2)]


def row_reduce_scatter(tokens, weights, n_row, after):
    n_y = n_row // 2
    r = lax.axis_index("row")
    y = r // 2
    core = r % 2
    rows = tokens.shape[0]
    halves = tokens.reshape(2, rows // 2, tokens.shape[1])
    send = lax.dynamic_index_in_dim(halves, 1 - core, 0, keepdims=False)
    keep = lax.dynamic_index_in_dim(halves, core, 0, keepdims=False)
    swap = [(i, i ^ 1) for i in range(n_row)]
    chunk = rows // 2 // n_y
    sent = []
    for w in weights:
        part = jnp.dot(send, w, preferred_element_type=jnp.float32).astype(jnp.bfloat16)
        sent.append(lax.ppermute(part, "row", swap))
    results = []
    for direction, w, got in ((1, weights[0], sent[0]), (-1, weights[1], sent[1])):
        mine = jnp.dot(keep, w, preferred_element_type=jnp.float32).astype(jnp.bfloat16)
        mine = lax.optimization_barrier(mine).reshape(n_y, chunk, w.shape[1])
        got = got.reshape(n_y, chunk, w.shape[1])

        def own(index, mine=mine, got=got):
            return (
                lax.dynamic_index_in_dim(mine, index, 0, keepdims=False).astype(jnp.float32)
                + lax.dynamic_index_in_dim(got, index, 0, keepdims=False).astype(jnp.float32)
            )

        pieces = []
        for sub in range(SUB_RINGS):
            rows_of = slice(sub * chunk // SUB_RINGS, (sub + 1) * chunk // SUB_RINGS)
            index = (y - direction) % n_y
            acc = own(index)[rows_of]
            if sub > 0:
                acc, lead = lax.optimization_barrier((acc, lead))
            for step in range(n_y - 1):
                received = lax.ppermute(
                    acc.astype(jnp.bfloat16), "row", row_perm(n_row, direction)
                )
                if step == 0:
                    lead = received
                index = (index - direction) % n_y
                acc = received.astype(jnp.float32) + own(index)[rows_of]
            pieces.append(acc)
        results.append(jnp.concatenate(pieces, axis=0))
    return results


def row_all_gather(value, n_row, down):
    n_y = n_row // 2
    r = lax.axis_index("row")
    y = r // 2
    core = r % 2
    chunk, width = value.shape
    parts = []
    for direction, cols in ((1, slice(0, width // 2)), (-1, slice(width // 2, width))):
        held = value[:, cols]
        full = jnp.zeros((n_y, chunk, width // 2), value.dtype)
        full = lax.dynamic_update_index_in_dim(full, held, y, 0)
        for step in range(n_y - 1):
            held = lax.ppermute(held, "row", row_perm(n_row, direction))
            full = lax.dynamic_update_index_in_dim(full, held, (y - direction * (step + 1)) % n_y, 0)
        parts.append(full)
    half = jnp.concatenate(parts, axis=2).reshape(n_y * chunk, width)
    swap = [(i, i ^ 1) for i in range(n_row)]
    other = lax.ppermute(half, "row", swap)
    mine = jnp.dot(half, down, preferred_element_type=jnp.float32).astype(jnp.bfloat16)
    theirs = jnp.dot(other, down, preferred_element_type=jnp.float32).astype(jnp.bfloat16)
    both = jnp.zeros((2, n_y * chunk, down.shape[1]), jnp.bfloat16)
    both = lax.dynamic_update_index_in_dim(both, mine, core, 0)
    both = lax.dynamic_update_index_in_dim(both, theirs, 1 - core, 0)
    return both.reshape(2 * n_y * chunk, down.shape[1])


def ring_reduce_scatter(own, pos, n, perm_of):
    width = own.shape[2]
    halves = []
    for direction, cols in ((1, slice(0, width // 2)), (-1, slice(width // 2, width))):
        part = own[:, :, cols]
        index = (pos - direction) % n
        acc = lax.dynamic_index_in_dim(part, index, 0, keepdims=False).astype(jnp.float32)
        for step in range(n - 1):
            got = lax.ppermute(acc.astype(jnp.bfloat16), "col", perm_of(direction))
            index = (index - direction) % n
            acc = got.astype(jnp.float32) + lax.dynamic_index_in_dim(part, index, 0, keepdims=False)
        halves.append(acc)
    return jnp.concatenate(halves, axis=1)


def ring_all_gather(value, pos, n, perm_of):
    chunk, width = value.shape
    parts = []
    for direction, cols in ((1, slice(0, width // 2)), (-1, slice(width // 2, width))):
        held = value[:, cols]
        full = jnp.zeros((n, chunk, width // 2), value.dtype)
        full = lax.dynamic_update_index_in_dim(full, held, pos, 0)
        for step in range(n - 1):
            held = lax.ppermute(held, "col", perm_of(direction))
            full = lax.dynamic_update_index_in_dim(full, held, (pos - direction * (step + 1)) % n, 0)
        parts.append(full)
    return jnp.concatenate(parts, axis=2)


def col_axes(n_col):
    n_z = 4 if n_col % 4 == 0 else 1
    n_x = n_col // n_z
    c = lax.axis_index("col")

    def x_perm(d):
        return [(i * n_z + j, ((i + d) % n_x) * n_z + j) for i in range(n_x) for j in range(n_z)]

    def z_perm(d):
        return [(i * n_z + j, i * n_z + (j + d) % n_z) for i in range(n_x) for j in range(n_z)]

    return n_x, n_z, c // n_z, c % n_z, x_perm, z_perm


def col_all_gather(value, n_col):
    n_x, n_z, x, z, x_perm, z_perm = col_axes(n_col)
    rows, width = value.shape
    part = ring_all_gather(value, z, n_z, z_perm).reshape(n_z * rows, width)
    return ring_all_gather(part, x, n_x, x_perm).reshape(n_x * n_z * rows, width)


def col_reduce_scatter(terms, n_col):
    n_z = 4 if n_col % 4 == 0 else 1
    n_x = n_col // n_z
    c = lax.axis_index("col")
    x = c // n_z
    z = c % n_z
    rows, width = terms.shape

    def x_perm(d):
        return [(i * n_z + j, ((i + d) % n_x) * n_z + j) for i in range(n_x) for j in range(n_z)]

    def z_perm(d):
        return [(i * n_z + j, i * n_z + (j + d) % n_z) for i in range(n_x) for j in range(n_z)]

    part = ring_reduce_scatter(terms.reshape(n_x, rows // n_x, width), x, n_x, x_perm)
    part = part.astype(jnp.bfloat16).reshape(n_z, rows // n_x // n_z, width)
    return ring_reduce_scatter(part, z, n_z, z_perm).astype(jnp.bfloat16)


def on_device(
    tokens,
    gate_weight,
    up_weight,
    down_weight,
    gate_keep,
    gate_count,
    up_keep,
    up_count,
    down_keep,
    down_count,
):
    model_blocks = gate_weight.shape[0] // BLOCK
    hidden_blocks = gate_weight.shape[1] // BLOCK
    n_col = lax.axis_size("col")
    n_row = lax.axis_size("row")
    row_offset = lax.axis_index("row") * model_blocks
    col_offset = lax.axis_index("col") * hidden_blocks
    gate_pruned = apply_mask(
        gate_weight, local_mask(gate_keep, gate_count, row_offset, model_blocks).T, BLOCK
    )
    up_pruned = apply_mask(
        up_weight, local_mask(up_keep, up_count, row_offset, model_blocks).T, BLOCK
    )
    down_pruned = apply_mask(
        down_weight, local_mask(down_keep, down_count, col_offset, hidden_blocks).T, BLOCK
    )
    rows = tokens.shape[0] // CHUNKS
    gathered = lax.all_gather(tokens, "col", axis=0, tiled=True)
    gathered = gathered.reshape(n_col, CHUNKS, rows, gathered.shape[1])
    outs = []
    previous = None
    for k in range(CHUNKS):
        chunk = gathered[:, k].reshape(n_col * rows, gathered.shape[3])
        gate_sums, up_sums = row_reduce_scatter(chunk, (gate_pruned, up_pruned), n_row, previous)
        hidden = (jax.nn.silu(gate_sums) * up_sums).astype(jnp.bfloat16)
        terms = row_all_gather(hidden, n_row, down_pruned)
        previous = terms
        if COL_RING:
            outs.append(col_reduce_scatter(terms, n_col))
        elif COL_A2A and k == CHUNKS - 1:
            terms = terms.reshape(n_col, rows, terms.shape[1])
            terms = lax.all_to_all(terms, "col", 0, 0, tiled=False)
            outs.append(jnp.sum(terms.astype(jnp.float32), axis=0).astype(jnp.bfloat16))
        else:
            outs.append(lax.psum_scatter(terms, "col", scatter_dimension=0, tiled=True))
    return jnp.concatenate(outs, axis=0)


def solution(mesh):
    return jax.shard_map(
        on_device,
        mesh=mesh,
        in_specs=(
            P("col", "row"),
            P("row", "col"),
            P("row", "col"),
            P("col", "row"),
            P("col", None),
            P("col"),
            P("col", None),
            P("col"),
            P("row", None),
            P("row"),
        ),
        out_specs=P("col", "row"),
        check_vma=False,
    )
```

```python
import jax
import jax.numpy as jnp
from jax import lax
from jax.sharding import PartitionSpec as P

BLOCK = 128
CHUNKS = 1
COL_A2A = True
COL_RING = False
SUB_RINGS = 2


def local_mask(keep_list, keep_count, offset, blocks):
    position = jnp.arange(keep_list.shape[1], dtype=jnp.int32)
    active_slot = position[None, :] < keep_count[:, None]
    local_index = keep_list - offset
    matches = (
        local_index[:, :, None] == jnp.arange(blocks, dtype=jnp.int32)[None, None, :]
    ) & active_slot[:, :, None]
    return jnp.any(matches, axis=1)


def apply_mask(weight, block_mask, block_size):
    block_rows, block_cols = block_mask.shape
    shaped = weight.reshape(block_rows, block_size, block_cols, block_size)
    masked = jnp.where(block_mask[:, None, :, None], shaped, jnp.zeros((), weight.dtype))
    return masked.reshape(weight.shape)


def row_perm(n_row, step):
    n_y = n_row // 2
    return [(y * 2 + c, ((y + step) % n_y) * 2 + c) for y in range(n_y) for c in range(2)]


def row_reduce_scatter(tokens, weights, n_row, after):
    n_y = n_row // 2
    r = lax.axis_index("row")
    y = r // 2
    core = r % 2
    rows = tokens.shape[0]
    halves = tokens.reshape(2, rows // 2, tokens.shape[1])
    send = lax.dynamic_index_in_dim(halves, 1 - core, 0, keepdims=False)
    keep = lax.dynamic_index_in_dim(halves, core, 0, keepdims=False)
    swap = [(i, i ^ 1) for i in range(n_row)]
    chunk = rows // 2 // n_y
    sent = []
    for w in weights:
        part = jnp.dot(send, w, preferred_element_type=jnp.float32).astype(jnp.bfloat16)
        sent.append(lax.ppermute(part, "row", swap))
    results = []
    for direction, w, got in ((1, weights[0], sent[0]), (-1, weights[1], sent[1])):
        mine = jnp.dot(keep, w, preferred_element_type=jnp.float32).astype(jnp.bfloat16)
        mine = lax.optimization_barrier(mine).reshape(n_y, chunk, w.shape[1])
        got = got.reshape(n_y, chunk, w.shape[1])

        def own(index, mine=mine, got=got):
            return (
                lax.dynamic_index_in_dim(mine, index, 0, keepdims=False).astype(jnp.float32)
                + lax.dynamic_index_in_dim(got, index, 0, keepdims=False).astype(jnp.float32)
            )

        pieces = []
        leads = []
        for sub in range(SUB_RINGS):
            rows_of = slice(sub * chunk // SUB_RINGS, (sub + 1) * chunk // SUB_RINGS)
            index = (y - direction) % n_y
            acc = own(index)[rows_of]
            for step in range(n_y - 1):
                if sub > 0:
                    acc, _ = lax.optimization_barrier((acc, leads[step]))
                received = lax.ppermute(
                    acc.astype(jnp.bfloat16), "row", row_perm(n_row, direction)
                )
                if sub == 0:
                    leads.append(received)
                index = (index - direction) % n_y
                acc = received.astype(jnp.float32) + own(index)[rows_of]
            pieces.append(acc)
        results.append(jnp.concatenate(pieces, axis=0))
    return results


def row_all_gather(value, n_row, down):
    n_y = n_row // 2
    r = lax.axis_index("row")
    y = r // 2
    core = r % 2
    chunk, width = value.shape
    parts = []
    for direction, cols in ((1, slice(0, width // 2)), (-1, slice(width // 2, width))):
        held = value[:, cols]
        full = jnp.zeros((n_y, chunk, width // 2), value.dtype)
        full = lax.dynamic_update_index_in_dim(full, held, y, 0)
        for step in range(n_y - 1):
            held = lax.ppermute(held, "row", row_perm(n_row, direction))
            full = lax.dynamic_update_index_in_dim(full, held, (y - direction * (step + 1)) % n_y, 0)
        parts.append(full)
    half = jnp.concatenate(parts, axis=2).reshape(n_y * chunk, width)
    swap = [(i, i ^ 1) for i in range(n_row)]
    other = lax.ppermute(half, "row", swap)
    mine = jnp.dot(half, down, preferred_element_type=jnp.float32).astype(jnp.bfloat16)
    theirs = jnp.dot(other, down, preferred_element_type=jnp.float32).astype(jnp.bfloat16)
    both = jnp.zeros((2, n_y * chunk, down.shape[1]), jnp.bfloat16)
    both = lax.dynamic_update_index_in_dim(both, mine, core, 0)
    both = lax.dynamic_update_index_in_dim(both, theirs, 1 - core, 0)
    return both.reshape(2 * n_y * chunk, down.shape[1])


def ring_reduce_scatter(own, pos, n, perm_of):
    width = own.shape[2]
    halves = []
    for direction, cols in ((1, slice(0, width // 2)), (-1, slice(width // 2, width))):
        part = own[:, :, cols]
        index = (pos - direction) % n
        acc = lax.dynamic_index_in_dim(part, index, 0, keepdims=False).astype(jnp.float32)
        for step in range(n - 1):
            got = lax.ppermute(acc.astype(jnp.bfloat16), "col", perm_of(direction))
            index = (index - direction) % n
            acc = got.astype(jnp.float32) + lax.dynamic_index_in_dim(part, index, 0, keepdims=False)
        halves.append(acc)
    return jnp.concatenate(halves, axis=1)


def ring_all_gather(value, pos, n, perm_of):
    chunk, width = value.shape
    parts = []
    for direction, cols in ((1, slice(0, width // 2)), (-1, slice(width // 2, width))):
        held = value[:, cols]
        full = jnp.zeros((n, chunk, width // 2), value.dtype)
        full = lax.dynamic_update_index_in_dim(full, held, pos, 0)
        for step in range(n - 1):
            held = lax.ppermute(held, "col", perm_of(direction))
            full = lax.dynamic_update_index_in_dim(full, held, (pos - direction * (step + 1)) % n, 0)
        parts.append(full)
    return jnp.concatenate(parts, axis=2)


def col_axes(n_col):
    n_z = 4 if n_col % 4 == 0 else 1
    n_x = n_col // n_z
    c = lax.axis_index("col")

    def x_perm(d):
        return [(i * n_z + j, ((i + d) % n_x) * n_z + j) for i in range(n_x) for j in range(n_z)]

    def z_perm(d):
        return [(i * n_z + j, i * n_z + (j + d) % n_z) for i in range(n_x) for j in range(n_z)]

    return n_x, n_z, c // n_z, c % n_z, x_perm, z_perm


def col_all_gather(value, n_col):
    n_x, n_z, x, z, x_perm, z_perm = col_axes(n_col)
    rows, width = value.shape
    part = ring_all_gather(value, z, n_z, z_perm).reshape(n_z * rows, width)
    return ring_all_gather(part, x, n_x, x_perm).reshape(n_x * n_z * rows, width)


def col_reduce_scatter(terms, n_col):
    n_z = 4 if n_col % 4 == 0 else 1
    n_x = n_col // n_z
    c = lax.axis_index("col")
    x = c // n_z
    z = c % n_z
    rows, width = terms.shape

    def x_perm(d):
        return [(i * n_z + j, ((i + d) % n_x) * n_z + j) for i in range(n_x) for j in range(n_z)]

    def z_perm(d):
        return [(i * n_z + j, i * n_z + (j + d) % n_z) for i in range(n_x) for j in range(n_z)]

    part = ring_reduce_scatter(terms.reshape(n_x, rows // n_x, width), x, n_x, x_perm)
    part = part.astype(jnp.bfloat16).reshape(n_z, rows // n_x // n_z, width)
    return ring_reduce_scatter(part, z, n_z, z_perm).astype(jnp.bfloat16)


def on_device(
    tokens,
    gate_weight,
    up_weight,
    down_weight,
    gate_keep,
    gate_count,
    up_keep,
    up_count,
    down_keep,
    down_count,
):
    model_blocks = gate_weight.shape[0] // BLOCK
    hidden_blocks = gate_weight.shape[1] // BLOCK
    n_col = lax.axis_size("col")
    n_row = lax.axis_size("row")
    row_offset = lax.axis_index("row") * model_blocks
    col_offset = lax.axis_index("col") * hidden_blocks
    gate_pruned = apply_mask(
        gate_weight, local_mask(gate_keep, gate_count, row_offset, model_blocks).T, BLOCK
    )
    up_pruned = apply_mask(
        up_weight, local_mask(up_keep, up_count, row_offset, model_blocks).T, BLOCK
    )
    down_pruned = apply_mask(
        down_weight, local_mask(down_keep, down_count, col_offset, hidden_blocks).T, BLOCK
    )
    rows = tokens.shape[0] // CHUNKS
    gathered = lax.all_gather(tokens, "col", axis=0, tiled=True)
    gathered = gathered.reshape(n_col, CHUNKS, rows, gathered.shape[1])
    outs = []
    previous = None
    for k in range(CHUNKS):
        chunk = gathered[:, k].reshape(n_col * rows, gathered.shape[3])
        gate_sums, up_sums = row_reduce_scatter(chunk, (gate_pruned, up_pruned), n_row, previous)
        hidden = (jax.nn.silu(gate_sums) * up_sums).astype(jnp.bfloat16)
        terms = row_all_gather(hidden, n_row, down_pruned)
        previous = terms
        if COL_RING:
            outs.append(col_reduce_scatter(terms, n_col))
        elif COL_A2A and k == CHUNKS - 1:
            terms = terms.reshape(n_col, rows, terms.shape[1])
            terms = lax.all_to_all(terms, "col", 0, 0, tiled=False)
            outs.append(jnp.sum(terms.astype(jnp.float32), axis=0).astype(jnp.bfloat16))
        else:
            outs.append(lax.psum_scatter(terms, "col", scatter_dimension=0, tiled=True))
    return jnp.concatenate(outs, axis=0)


def solution(mesh):
    return jax.shard_map(
        on_device,
        mesh=mesh,
        in_specs=(
            P("col", "row"),
            P("row", "col"),
            P("row", "col"),
            P("col", "row"),
            P("col", None),
            P("col"),
            P("col", None),
            P("col"),
            P("row", None),
            P("row"),
        ),
        out_specs=P("col", "row"),
        check_vma=False,
    )
```

```python
import jax
import jax.numpy as jnp
from jax import lax
from jax.sharding import PartitionSpec as P

BLOCK = 128
CHUNKS = 1
COL_A2A = True
COL_RING = False
SUB_RINGS = 2


def local_mask(keep_list, keep_count, offset, blocks):
    position = jnp.arange(keep_list.shape[1], dtype=jnp.int32)
    active_slot = position[None, :] < keep_count[:, None]
    local_index = keep_list - offset
    matches = (
        local_index[:, :, None] == jnp.arange(blocks, dtype=jnp.int32)[None, None, :]
    ) & active_slot[:, :, None]
    return jnp.any(matches, axis=1)


def apply_mask(weight, block_mask, block_size):
    block_rows, block_cols = block_mask.shape
    shaped = weight.reshape(block_rows, block_size, block_cols, block_size)
    masked = jnp.where(block_mask[:, None, :, None], shaped, jnp.zeros((), weight.dtype))
    return masked.reshape(weight.shape)


def row_perm(n_row, step):
    n_y = n_row // 2
    return [(y * 2 + c, ((y + step) % n_y) * 2 + c) for y in range(n_y) for c in range(2)]


def row_reduce_scatter(tokens, weights, n_row, after):
    n_y = n_row // 2
    r = lax.axis_index("row")
    y = r // 2
    core = r % 2
    rows = tokens.shape[0]
    halves = tokens.reshape(2, rows // 2, tokens.shape[1])
    send = lax.dynamic_index_in_dim(halves, 1 - core, 0, keepdims=False)
    keep = lax.dynamic_index_in_dim(halves, core, 0, keepdims=False)
    swap = [(i, i ^ 1) for i in range(n_row)]
    chunk = rows // 2 // n_y
    sent = []
    for w in weights:
        part = jnp.dot(send, w, preferred_element_type=jnp.float32).astype(jnp.bfloat16)
        sent.append(lax.ppermute(part, "row", swap))
    results = []
    for direction, w, got in ((1, weights[0], sent[0]), (-1, weights[1], sent[1])):
        mine = jnp.dot(keep, w, preferred_element_type=jnp.float32).astype(jnp.bfloat16)
        mine = lax.optimization_barrier(mine).reshape(n_y, chunk, w.shape[1])
        got = got.reshape(n_y, chunk, w.shape[1])

        def own(index, mine=mine, got=got):
            return (
                lax.dynamic_index_in_dim(mine, index, 0, keepdims=False).astype(jnp.float32)
                + lax.dynamic_index_in_dim(got, index, 0, keepdims=False).astype(jnp.float32)
            )

        pieces = []
        leads = []
        for sub in range(SUB_RINGS):
            rows_of = slice(sub * chunk // SUB_RINGS, (sub + 1) * chunk // SUB_RINGS)
            index = (y - direction) % n_y
            acc = own(index)[rows_of]
            for step in range(n_y - 1):
                if sub > 0:
                    acc, _ = lax.optimization_barrier((acc, leads[step]))
                received = lax.ppermute(
                    acc.astype(jnp.bfloat16), "row", row_perm(n_row, direction)
                )
                if sub == 0:
                    leads.append(received)
                index = (index - direction) % n_y
                acc = received.astype(jnp.float32) + own(index)[rows_of]
            pieces.append(acc)
        results.append(jnp.concatenate(pieces, axis=0))
    return results


def row_all_gather(value, n_row, down):
    n_y = n_row // 2
    r = lax.axis_index("row")
    y = r // 2
    core = r % 2
    chunk, width = value.shape
    parts = []
    for direction, cols in ((1, slice(0, width // 2)), (-1, slice(width // 2, width))):
        full = jnp.zeros((n_y, chunk, width // 2), value.dtype)
        full = lax.dynamic_update_index_in_dim(full, value[:, cols], y, 0)
        leads = []
        for sub in range(SUB_RINGS):
            start = sub * chunk // SUB_RINGS
            held = value[start:start + chunk // SUB_RINGS, cols]
            for step in range(n_y - 1):
                if sub > 0:
                    held, _ = lax.optimization_barrier((held, leads[step]))
                held = lax.ppermute(held, "row", row_perm(n_row, direction))
                if sub == 0:
                    leads.append(held)
                place = (y - direction * (step + 1)) % n_y
                full = lax.dynamic_update_slice(full, held[None], (place, start, 0))
        parts.append(full)
    half = jnp.concatenate(parts, axis=2).reshape(n_y * chunk, width)
    swap = [(i, i ^ 1) for i in range(n_row)]
    other = lax.ppermute(half, "row", swap)
    mine = jnp.dot(half, down, preferred_element_type=jnp.float32).astype(jnp.bfloat16)
    theirs = jnp.dot(other, down, preferred_element_type=jnp.float32).astype(jnp.bfloat16)
    both = jnp.zeros((2, n_y * chunk, down.shape[1]), jnp.bfloat16)
    both = lax.dynamic_update_index_in_dim(both, mine, core, 0)
    both = lax.dynamic_update_index_in_dim(both, theirs, 1 - core, 0)
    return both.reshape(2 * n_y * chunk, down.shape[1])


def ring_reduce_scatter(own, pos, n, perm_of):
    width = own.shape[2]
    halves = []
    for direction, cols in ((1, slice(0, width // 2)), (-1, slice(width // 2, width))):
        part = own[:, :, cols]
        index = (pos - direction) % n
        acc = lax.dynamic_index_in_dim(part, index, 0, keepdims=False).astype(jnp.float32)
        for step in range(n - 1):
            got = lax.ppermute(acc.astype(jnp.bfloat16), "col", perm_of(direction))
            index = (index - direction) % n
            acc = got.astype(jnp.float32) + lax.dynamic_index_in_dim(part, index, 0, keepdims=False)
        halves.append(acc)
    return jnp.concatenate(halves, axis=1)


def ring_all_gather(value, pos, n, perm_of):
    chunk, width = value.shape
    parts = []
    for direction, cols in ((1, slice(0, width // 2)), (-1, slice(width // 2, width))):
        held = value[:, cols]
        full = jnp.zeros((n, chunk, width // 2), value.dtype)
        full = lax.dynamic_update_index_in_dim(full, held, pos, 0)
        for step in range(n - 1):
            held = lax.ppermute(held, "col", perm_of(direction))
            full = lax.dynamic_update_index_in_dim(full, held, (pos - direction * (step + 1)) % n, 0)
        parts.append(full)
    return jnp.concatenate(parts, axis=2)


def col_axes(n_col):
    n_z = 4 if n_col % 4 == 0 else 1
    n_x = n_col // n_z
    c = lax.axis_index("col")

    def x_perm(d):
        return [(i * n_z + j, ((i + d) % n_x) * n_z + j) for i in range(n_x) for j in range(n_z)]

    def z_perm(d):
        return [(i * n_z + j, i * n_z + (j + d) % n_z) for i in range(n_x) for j in range(n_z)]

    return n_x, n_z, c // n_z, c % n_z, x_perm, z_perm


def col_all_gather(value, n_col):
    n_x, n_z, x, z, x_perm, z_perm = col_axes(n_col)
    rows, width = value.shape
    part = ring_all_gather(value, z, n_z, z_perm).reshape(n_z * rows, width)
    return ring_all_gather(part, x, n_x, x_perm).reshape(n_x * n_z * rows, width)


def col_reduce_scatter(terms, n_col):
    n_z = 4 if n_col % 4 == 0 else 1
    n_x = n_col // n_z
    c = lax.axis_index("col")
    x = c // n_z
    z = c % n_z
    rows, width = terms.shape

    def x_perm(d):
        return [(i * n_z + j, ((i + d) % n_x) * n_z + j) for i in range(n_x) for j in range(n_z)]

    def z_perm(d):
        return [(i * n_z + j, i * n_z + (j + d) % n_z) for i in range(n_x) for j in range(n_z)]

    part = ring_reduce_scatter(terms.reshape(n_x, rows // n_x, width), x, n_x, x_perm)
    part = part.astype(jnp.bfloat16).reshape(n_z, rows // n_x // n_z, width)
    return ring_reduce_scatter(part, z, n_z, z_perm).astype(jnp.bfloat16)


def on_device(
    tokens,
    gate_weight,
    up_weight,
    down_weight,
    gate_keep,
    gate_count,
    up_keep,
    up_count,
    down_keep,
    down_count,
):
    model_blocks = gate_weight.shape[0] // BLOCK
    hidden_blocks = gate_weight.shape[1] // BLOCK
    n_col = lax.axis_size("col")
    n_row = lax.axis_size("row")
    row_offset = lax.axis_index("row") * model_blocks
    col_offset = lax.axis_index("col") * hidden_blocks
    gate_pruned = apply_mask(
        gate_weight, local_mask(gate_keep, gate_count, row_offset, model_blocks).T, BLOCK
    )
    up_pruned = apply_mask(
        up_weight, local_mask(up_keep, up_count, row_offset, model_blocks).T, BLOCK
    )
    down_pruned = apply_mask(
        down_weight, local_mask(down_keep, down_count, col_offset, hidden_blocks).T, BLOCK
    )
    rows = tokens.shape[0] // CHUNKS
    gathered = lax.all_gather(tokens, "col", axis=0, tiled=True)
    gathered = gathered.reshape(n_col, CHUNKS, rows, gathered.shape[1])
    outs = []
    previous = None
    for k in range(CHUNKS):
        chunk = gathered[:, k].reshape(n_col * rows, gathered.shape[3])
        gate_sums, up_sums = row_reduce_scatter(chunk, (gate_pruned, up_pruned), n_row, previous)
        hidden = (jax.nn.silu(gate_sums) * up_sums).astype(jnp.bfloat16)
        terms = row_all_gather(hidden, n_row, down_pruned)
        previous = terms
        if COL_RING:
            outs.append(col_reduce_scatter(terms, n_col))
        elif COL_A2A and k == CHUNKS - 1:
            terms = terms.reshape(n_col, rows, terms.shape[1])
            terms = lax.all_to_all(terms, "col", 0, 0, tiled=False)
            outs.append(jnp.sum(terms.astype(jnp.float32), axis=0).astype(jnp.bfloat16))
        else:
            outs.append(lax.psum_scatter(terms, "col", scatter_dimension=0, tiled=True))
    return jnp.concatenate(outs, axis=0)


def solution(mesh):
    return jax.shard_map(
        on_device,
        mesh=mesh,
        in_specs=(
            P("col", "row"),
            P("row", "col"),
            P("row", "col"),
            P("col", "row"),
            P("col", None),
            P("col"),
            P("col", None),
            P("col"),
            P("row", None),
            P("row"),
        ),
        out_specs=P("col", "row"),
        check_vma=False,
    )
```

```python
import jax
import jax.numpy as jnp
from jax import lax
from jax.sharding import PartitionSpec as P

BLOCK = 128
CHUNKS = 1
COL_A2A = True
COL_RING = False
SUB_RINGS = 4


def local_mask(keep_list, keep_count, offset, blocks):
    position = jnp.arange(keep_list.shape[1], dtype=jnp.int32)
    active_slot = position[None, :] < keep_count[:, None]
    local_index = keep_list - offset
    matches = (
        local_index[:, :, None] == jnp.arange(blocks, dtype=jnp.int32)[None, None, :]
    ) & active_slot[:, :, None]
    return jnp.any(matches, axis=1)


def apply_mask(weight, block_mask, block_size):
    block_rows, block_cols = block_mask.shape
    shaped = weight.reshape(block_rows, block_size, block_cols, block_size)
    masked = jnp.where(block_mask[:, None, :, None], shaped, jnp.zeros((), weight.dtype))
    return masked.reshape(weight.shape)


def row_perm(n_row, step):
    n_y = n_row // 2
    return [(y * 2 + c, ((y + step) % n_y) * 2 + c) for y in range(n_y) for c in range(2)]


def row_reduce_scatter(tokens, weights, n_row, after):
    n_y = n_row // 2
    r = lax.axis_index("row")
    y = r // 2
    core = r % 2
    rows = tokens.shape[0]
    halves = tokens.reshape(2, rows // 2, tokens.shape[1])
    send = lax.dynamic_index_in_dim(halves, 1 - core, 0, keepdims=False)
    keep = lax.dynamic_index_in_dim(halves, core, 0, keepdims=False)
    swap = [(i, i ^ 1) for i in range(n_row)]
    chunk = rows // 2 // n_y
    sent = []
    for w in weights:
        part = jnp.dot(send, w, preferred_element_type=jnp.float32).astype(jnp.bfloat16)
        sent.append(lax.ppermute(part, "row", swap))
    results = []
    for direction, w, got in ((1, weights[0], sent[0]), (-1, weights[1], sent[1])):
        mine = jnp.dot(keep, w, preferred_element_type=jnp.float32).astype(jnp.bfloat16)
        mine = lax.optimization_barrier(mine).reshape(n_y, chunk, w.shape[1])
        got = got.reshape(n_y, chunk, w.shape[1])

        def own(index, mine=mine, got=got):
            return (
                lax.dynamic_index_in_dim(mine, index, 0, keepdims=False).astype(jnp.float32)
                + lax.dynamic_index_in_dim(got, index, 0, keepdims=False).astype(jnp.float32)
            )

        pieces = []
        leads = []
        for sub in range(SUB_RINGS):
            rows_of = slice(sub * chunk // SUB_RINGS, (sub + 1) * chunk // SUB_RINGS)
            index = (y - direction) % n_y
            acc = own(index)[rows_of]
            for step in range(n_y - 1):
                if sub > 0:
                    acc, _ = lax.optimization_barrier((acc, leads[step]))
                received = lax.ppermute(
                    acc.astype(jnp.bfloat16), "row", row_perm(n_row, direction)
                )
                if sub == 0:
                    leads.append(received)
                index = (index - direction) % n_y
                acc = received.astype(jnp.float32) + own(index)[rows_of]
            pieces.append(acc)
        results.append(jnp.concatenate(pieces, axis=0))
    return results


def row_all_gather(value, n_row, down):
    n_y = n_row // 2
    r = lax.axis_index("row")
    y = r // 2
    core = r % 2
    chunk, width = value.shape
    parts = []
    for direction, cols in ((1, slice(0, width // 2)), (-1, slice(width // 2, width))):
        held = value[:, cols]
        full = jnp.zeros((n_y, chunk, width // 2), value.dtype)
        full = lax.dynamic_update_index_in_dim(full, held, y, 0)
        for step in range(n_y - 1):
            held = lax.ppermute(held, "row", row_perm(n_row, direction))
            full = lax.dynamic_update_index_in_dim(full, held, (y - direction * (step + 1)) % n_y, 0)
        parts.append(full)
    half = jnp.concatenate(parts, axis=2).reshape(n_y * chunk, width)
    swap = [(i, i ^ 1) for i in range(n_row)]
    other = lax.ppermute(half, "row", swap)
    mine = jnp.dot(half, down, preferred_element_type=jnp.float32).astype(jnp.bfloat16)
    theirs = jnp.dot(other, down, preferred_element_type=jnp.float32).astype(jnp.bfloat16)
    both = jnp.zeros((2, n_y * chunk, down.shape[1]), jnp.bfloat16)
    both = lax.dynamic_update_index_in_dim(both, mine, core, 0)
    both = lax.dynamic_update_index_in_dim(both, theirs, 1 - core, 0)
    return both.reshape(2 * n_y * chunk, down.shape[1])


def ring_reduce_scatter(own, pos, n, perm_of):
    width = own.shape[2]
    halves = []
    for direction, cols in ((1, slice(0, width // 2)), (-1, slice(width // 2, width))):
        part = own[:, :, cols]
        index = (pos - direction) % n
        acc = lax.dynamic_index_in_dim(part, index, 0, keepdims=False).astype(jnp.float32)
        for step in range(n - 1):
            got = lax.ppermute(acc.astype(jnp.bfloat16), "col", perm_of(direction))
            index = (index - direction) % n
            acc = got.astype(jnp.float32) + lax.dynamic_index_in_dim(part, index, 0, keepdims=False)
        halves.append(acc)
    return jnp.concatenate(halves, axis=1)


def ring_all_gather(value, pos, n, perm_of):
    chunk, width = value.shape
    parts = []
    for direction, cols in ((1, slice(0, width // 2)), (-1, slice(width // 2, width))):
        held = value[:, cols]
        full = jnp.zeros((n, chunk, width // 2), value.dtype)
        full = lax.dynamic_update_index_in_dim(full, held, pos, 0)
        for step in range(n - 1):
            held = lax.ppermute(held, "col", perm_of(direction))
            full = lax.dynamic_update_index_in_dim(full, held, (pos - direction * (step + 1)) % n, 0)
        parts.append(full)
    return jnp.concatenate(parts, axis=2)


def col_axes(n_col):
    n_z = 4 if n_col % 4 == 0 else 1
    n_x = n_col // n_z
    c = lax.axis_index("col")

    def x_perm(d):
        return [(i * n_z + j, ((i + d) % n_x) * n_z + j) for i in range(n_x) for j in range(n_z)]

    def z_perm(d):
        return [(i * n_z + j, i * n_z + (j + d) % n_z) for i in range(n_x) for j in range(n_z)]

    return n_x, n_z, c // n_z, c % n_z, x_perm, z_perm


def col_all_gather(value, n_col):
    n_x, n_z, x, z, x_perm, z_perm = col_axes(n_col)
    rows, width = value.shape
    part = ring_all_gather(value, z, n_z, z_perm).reshape(n_z * rows, width)
    return ring_all_gather(part, x, n_x, x_perm).reshape(n_x * n_z * rows, width)


def col_reduce_scatter(terms, n_col):
    n_z = 4 if n_col % 4 == 0 else 1
    n_x = n_col // n_z
    c = lax.axis_index("col")
    x = c // n_z
    z = c % n_z
    rows, width = terms.shape

    def x_perm(d):
        return [(i * n_z + j, ((i + d) % n_x) * n_z + j) for i in range(n_x) for j in range(n_z)]

    def z_perm(d):
        return [(i * n_z + j, i * n_z + (j + d) % n_z) for i in range(n_x) for j in range(n_z)]

    part = ring_reduce_scatter(terms.reshape(n_x, rows // n_x, width), x, n_x, x_perm)
    part = part.astype(jnp.bfloat16).reshape(n_z, rows // n_x // n_z, width)
    return ring_reduce_scatter(part, z, n_z, z_perm).astype(jnp.bfloat16)


def on_device(
    tokens,
    gate_weight,
    up_weight,
    down_weight,
    gate_keep,
    gate_count,
    up_keep,
    up_count,
    down_keep,
    down_count,
):
    model_blocks = gate_weight.shape[0] // BLOCK
    hidden_blocks = gate_weight.shape[1] // BLOCK
    n_col = lax.axis_size("col")
    n_row = lax.axis_size("row")
    row_offset = lax.axis_index("row") * model_blocks
    col_offset = lax.axis_index("col") * hidden_blocks
    gate_pruned = apply_mask(
        gate_weight, local_mask(gate_keep, gate_count, row_offset, model_blocks).T, BLOCK
    )
    up_pruned = apply_mask(
        up_weight, local_mask(up_keep, up_count, row_offset, model_blocks).T, BLOCK
    )
    down_pruned = apply_mask(
        down_weight, local_mask(down_keep, down_count, col_offset, hidden_blocks).T, BLOCK
    )
    rows = tokens.shape[0] // CHUNKS
    gathered = lax.all_gather(tokens, "col", axis=0, tiled=True)
    gathered = gathered.reshape(n_col, CHUNKS, rows, gathered.shape[1])
    outs = []
    previous = None
    for k in range(CHUNKS):
        chunk = gathered[:, k].reshape(n_col * rows, gathered.shape[3])
        gate_sums, up_sums = row_reduce_scatter(chunk, (gate_pruned, up_pruned), n_row, previous)
        hidden = (jax.nn.silu(gate_sums) * up_sums).astype(jnp.bfloat16)
        terms = row_all_gather(hidden, n_row, down_pruned)
        previous = terms
        if COL_RING:
            outs.append(col_reduce_scatter(terms, n_col))
        elif COL_A2A and k == CHUNKS - 1:
            terms = terms.reshape(n_col, rows, terms.shape[1])
            terms = lax.all_to_all(terms, "col", 0, 0, tiled=False)
            outs.append(jnp.sum(terms.astype(jnp.float32), axis=0).astype(jnp.bfloat16))
        else:
            outs.append(lax.psum_scatter(terms, "col", scatter_dimension=0, tiled=True))
    return jnp.concatenate(outs, axis=0)


def solution(mesh):
    return jax.shard_map(
        on_device,
        mesh=mesh,
        in_specs=(
            P("col", "row"),
            P("row", "col"),
            P("row", "col"),
            P("col", "row"),
            P("col", None),
            P("col"),
            P("col", None),
            P("col"),
            P("row", None),
            P("row"),
        ),
        out_specs=P("col", "row"),
        check_vma=False,
    )
```

```python
import jax
import jax.numpy as jnp
from jax import lax
from jax.sharding import PartitionSpec as P

BLOCK = 128
CHUNKS = 1
COL_A2A = True
COL_RING = False
SUB_RINGS = 2


def local_mask(keep_list, keep_count, offset, blocks):
    position = jnp.arange(keep_list.shape[1], dtype=jnp.int32)
    active_slot = position[None, :] < keep_count[:, None]
    local_index = keep_list - offset
    matches = (
        local_index[:, :, None] == jnp.arange(blocks, dtype=jnp.int32)[None, None, :]
    ) & active_slot[:, :, None]
    return jnp.any(matches, axis=1)


def apply_mask(weight, block_mask, block_size):
    block_rows, block_cols = block_mask.shape
    shaped = weight.reshape(block_rows, block_size, block_cols, block_size)
    masked = jnp.where(block_mask[:, None, :, None], shaped, jnp.zeros((), weight.dtype))
    return masked.reshape(weight.shape)


def row_perm(n_row, step):
    n_y = n_row // 2
    return [(y * 2 + c, ((y + step) % n_y) * 2 + c) for y in range(n_y) for c in range(2)]


def row_reduce_scatter(tokens, weights, n_row, after):
    n_y = n_row // 2
    r = lax.axis_index("row")
    y = r // 2
    core = r % 2
    rows = tokens.shape[0]
    halves = tokens.reshape(2, rows // 2, tokens.shape[1])
    send = lax.dynamic_index_in_dim(halves, 1 - core, 0, keepdims=False)
    keep = lax.dynamic_index_in_dim(halves, core, 0, keepdims=False)
    swap = [(i, i ^ 1) for i in range(n_row)]
    chunk = rows // 2 // n_y
    sent = []
    for w in weights:
        part = jnp.dot(send, w, preferred_element_type=jnp.float32).astype(jnp.bfloat16)
        sent.append(lax.ppermute(part, "row", swap))
    results = []
    for direction, w, got in ((1, weights[0], sent[0]), (-1, weights[1], sent[1])):
        mine = jnp.dot(keep, w, preferred_element_type=jnp.float32).astype(jnp.bfloat16)
        mine = lax.optimization_barrier(mine).reshape(n_y, chunk, w.shape[1])
        got = got.reshape(n_y, chunk, w.shape[1])

        def own(index, mine=mine, got=got):
            return (
                lax.dynamic_index_in_dim(mine, index, 0, keepdims=False).astype(jnp.float32)
                + lax.dynamic_index_in_dim(got, index, 0, keepdims=False).astype(jnp.float32)
            )

        pieces = []
        leads = []
        for sub in range(SUB_RINGS):
            rows_of = slice(sub * chunk // SUB_RINGS, (sub + 1) * chunk // SUB_RINGS)
            index = (y - direction) % n_y
            acc = own(index)[rows_of]
            for step in range(n_y - 1):
                if sub > 0:
                    acc, _ = lax.optimization_barrier((acc, leads[step]))
                elif direction < 0:
                    acc, _ = lax.optimization_barrier((acc, first_leads[step]))
                received = lax.ppermute(
                    acc.astype(jnp.bfloat16), "row", row_perm(n_row, direction)
                )
                if sub == 0:
                    leads.append(received)
                index = (index - direction) % n_y
                acc = received.astype(jnp.float32) + own(index)[rows_of]
            pieces.append(acc)
        first_leads = leads
        results.append(jnp.concatenate(pieces, axis=0))
    return results


def row_all_gather(value, n_row, down):
    n_y = n_row // 2
    r = lax.axis_index("row")
    y = r // 2
    core = r % 2
    chunk, width = value.shape
    parts = []
    for direction, cols in ((1, slice(0, width // 2)), (-1, slice(width // 2, width))):
        held = value[:, cols]
        full = jnp.zeros((n_y, chunk, width // 2), value.dtype)
        full = lax.dynamic_update_index_in_dim(full, held, y, 0)
        for step in range(n_y - 1):
            held = lax.ppermute(held, "row", row_perm(n_row, direction))
            full = lax.dynamic_update_index_in_dim(full, held, (y - direction * (step + 1)) % n_y, 0)
        parts.append(full)
    half = jnp.concatenate(parts, axis=2).reshape(n_y * chunk, width)
    swap = [(i, i ^ 1) for i in range(n_row)]
    other = lax.ppermute(half, "row", swap)
    mine = jnp.dot(half, down, preferred_element_type=jnp.float32).astype(jnp.bfloat16)
    theirs = jnp.dot(other, down, preferred_element_type=jnp.float32).astype(jnp.bfloat16)
    both = jnp.zeros((2, n_y * chunk, down.shape[1]), jnp.bfloat16)
    both = lax.dynamic_update_index_in_dim(both, mine, core, 0)
    both = lax.dynamic_update_index_in_dim(both, theirs, 1 - core, 0)
    return both.reshape(2 * n_y * chunk, down.shape[1])


def ring_reduce_scatter(own, pos, n, perm_of):
    width = own.shape[2]
    halves = []
    for direction, cols in ((1, slice(0, width // 2)), (-1, slice(width // 2, width))):
        part = own[:, :, cols]
        index = (pos - direction) % n
        acc = lax.dynamic_index_in_dim(part, index, 0, keepdims=False).astype(jnp.float32)
        for step in range(n - 1):
            got = lax.ppermute(acc.astype(jnp.bfloat16), "col", perm_of(direction))
            index = (index - direction) % n
            acc = got.astype(jnp.float32) + lax.dynamic_index_in_dim(part, index, 0, keepdims=False)
        halves.append(acc)
    return jnp.concatenate(halves, axis=1)


def ring_all_gather(value, pos, n, perm_of):
    chunk, width = value.shape
    parts = []
    for direction, cols in ((1, slice(0, width // 2)), (-1, slice(width // 2, width))):
        held = value[:, cols]
        full = jnp.zeros((n, chunk, width // 2), value.dtype)
        full = lax.dynamic_update_index_in_dim(full, held, pos, 0)
        for step in range(n - 1):
            held = lax.ppermute(held, "col", perm_of(direction))
            full = lax.dynamic_update_index_in_dim(full, held, (pos - direction * (step + 1)) % n, 0)
        parts.append(full)
    return jnp.concatenate(parts, axis=2)


def col_axes(n_col):
    n_z = 4 if n_col % 4 == 0 else 1
    n_x = n_col // n_z
    c = lax.axis_index("col")

    def x_perm(d):
        return [(i * n_z + j, ((i + d) % n_x) * n_z + j) for i in range(n_x) for j in range(n_z)]

    def z_perm(d):
        return [(i * n_z + j, i * n_z + (j + d) % n_z) for i in range(n_x) for j in range(n_z)]

    return n_x, n_z, c // n_z, c % n_z, x_perm, z_perm


def col_all_gather(value, n_col):
    n_x, n_z, x, z, x_perm, z_perm = col_axes(n_col)
    rows, width = value.shape
    part = ring_all_gather(value, z, n_z, z_perm).reshape(n_z * rows, width)
    return ring_all_gather(part, x, n_x, x_perm).reshape(n_x * n_z * rows, width)


def col_reduce_scatter(terms, n_col):
    n_z = 4 if n_col % 4 == 0 else 1
    n_x = n_col // n_z
    c = lax.axis_index("col")
    x = c // n_z
    z = c % n_z
    rows, width = terms.shape

    def x_perm(d):
        return [(i * n_z + j, ((i + d) % n_x) * n_z + j) for i in range(n_x) for j in range(n_z)]

    def z_perm(d):
        return [(i * n_z + j, i * n_z + (j + d) % n_z) for i in range(n_x) for j in range(n_z)]

    part = ring_reduce_scatter(terms.reshape(n_x, rows // n_x, width), x, n_x, x_perm)
    part = part.astype(jnp.bfloat16).reshape(n_z, rows // n_x // n_z, width)
    return ring_reduce_scatter(part, z, n_z, z_perm).astype(jnp.bfloat16)


def on_device(
    tokens,
    gate_weight,
    up_weight,
    down_weight,
    gate_keep,
    gate_count,
    up_keep,
    up_count,
    down_keep,
    down_count,
):
    model_blocks = gate_weight.shape[0] // BLOCK
    hidden_blocks = gate_weight.shape[1] // BLOCK
    n_col = lax.axis_size("col")
    n_row = lax.axis_size("row")
    row_offset = lax.axis_index("row") * model_blocks
    col_offset = lax.axis_index("col") * hidden_blocks
    gate_pruned = apply_mask(
        gate_weight, local_mask(gate_keep, gate_count, row_offset, model_blocks).T, BLOCK
    )
    up_pruned = apply_mask(
        up_weight, local_mask(up_keep, up_count, row_offset, model_blocks).T, BLOCK
    )
    down_pruned = apply_mask(
        down_weight, local_mask(down_keep, down_count, col_offset, hidden_blocks).T, BLOCK
    )
    rows = tokens.shape[0] // CHUNKS
    gathered = lax.all_gather(tokens, "col", axis=0, tiled=True)
    gathered = gathered.reshape(n_col, CHUNKS, rows, gathered.shape[1])
    outs = []
    previous = None
    for k in range(CHUNKS):
        chunk = gathered[:, k].reshape(n_col * rows, gathered.shape[3])
        gate_sums, up_sums = row_reduce_scatter(chunk, (gate_pruned, up_pruned), n_row, previous)
        hidden = (jax.nn.silu(gate_sums) * up_sums).astype(jnp.bfloat16)
        terms = row_all_gather(hidden, n_row, down_pruned)
        previous = terms
        if COL_RING:
            outs.append(col_reduce_scatter(terms, n_col))
        elif COL_A2A and k == CHUNKS - 1:
            terms = terms.reshape(n_col, rows, terms.shape[1])
            terms = lax.all_to_all(terms, "col", 0, 0, tiled=False)
            outs.append(jnp.sum(terms.astype(jnp.float32), axis=0).astype(jnp.bfloat16))
        else:
            outs.append(lax.psum_scatter(terms, "col", scatter_dimension=0, tiled=True))
    return jnp.concatenate(outs, axis=0)


def solution(mesh):
    return jax.shard_map(
        on_device,
        mesh=mesh,
        in_specs=(
            P("col", "row"),
            P("row", "col"),
            P("row", "col"),
            P("col", "row"),
            P("col", None),
            P("col"),
            P("col", None),
            P("col"),
            P("row", None),
            P("row"),
        ),
        out_specs=P("col", "row"),
        check_vma=False,
    )
```
